32 devices in a mesh: az: 16 (over z, y, x), wn: 2 (over core).
Axes of the slice: x: 2, y: 2, z: 4, core: 2. Of those that a mesh axis runs over, the one named last changes fastest.
Arguments:
- visc_wn: float32 [5, 32, 4096], P(None, 'wn', 'az'), may hold values from 0.5 to 2
- conv_wn: float32 [5, 5, 32, 4096], P(None, None, 'wn', 'az'), may hold values from -0.3 to 0.3
- spin: float32 [5, 5, 32, 4096], P(None, None, 'wn', 'az'), may hold values from -0.3 to 0.3
- visc_az: float32 [5, 32, 4096], P(None, 'wn', 'az'), may hold values from 0.001953125 to 0.015625
- flux_wn: float32 [5, 32, 4096], P(None, 'wn', 'az'), may hold values from -6 to 6
- flux_az: float32 [5, 32, 4096], P(None, 'wn', 'az'), may hold values from -0.375 to 0.375
- incr_prev: float32 [5, 32, 4096], P(None, 'wn', 'az'), may hold values from -12 to 12
- cell_type: int32 [32], P('wn'), may hold values from 0 to 1, as said below
- edge_index: int32 [4096], P('az'), may hold values from 8 to 23
Outputs:
- increment: float32 [5, 32, 4096], P(None, 'wn', 'az')
- defect: float32 [5, 32, 4096], P(None, 'wn', 'az')
The draws below stay inside these ranges and needn't reach their ends.
Inputs may be any that keep to these rules, and one draw needn't show every extreme that they name: cell_type is 1 exactly at the first t wall-normal points and 0 at the others, for one t from 2 to 4 in each draw.
All inputs are finite; a program needn't handle non-finite values.
Results may differ from the reference program's by a relative error of at most 0.0023.
Values sent between devices are 32-bit elements; how exact they have to be, the bound alone decides.
No kernel may reach another device: no remote copies, remote signals or barrier semaphores. Data moves between devices by JAX's collectives and lax.ppermute only.
A program may use at most 64 MiB of HBM per device.

```python
import math
import jax
import jax.numpy as jnp
from jax import lax

NC = 5
S = 8
AZ_DEV = 32
WN_DEV = 16
SWEEPS = 2
LINES = 4096
NW = 32


def draw_cell_type(key, part):
    thickness = jax.random.randint(key, (), WN_DEV // 8, WN_DEV // 4 + 1)
    return (jnp.arange(NW) < thickness).astype(jnp.int32)


def plant(values, key, low, largest):
    shape = values.shape
    place = [jax.random.randint(jax.random.fold_in(key, axis), (), 0, shape[axis]) for axis in range(len(shape))]
    values = values.at[tuple(place)].set(low)
    longest = shape.index(max(shape))
    place[longest] = (place[longest] + 1) % shape[longest]
    return values.at[tuple(place)].set(largest)


def block_levels(rng, dims, cuts, low, top_value):
    gain, own = 1.0, jax.random.fold_in(rng, 6)
    for dim, parts in cuts:
        heights = jnp.exp(jax.random.uniform(jax.random.fold_in(own, dim), (parts,), jnp.float32, low / len(cuts), top_value / len(cuts)))
        gain = gain * jnp.repeat(heights, dims[dim] // parts).reshape([-1 if axis == dim else 1 for axis in range(len(dims))])
    return gain


def centred(rng, shape, deviation, most, split=(), kind=jnp.bfloat16):
    loudness = block_levels(rng, shape, split, -0.22, 0.18) if split else 1.0
    array = jax.random.normal(rng, shape, jnp.float32) * deviation * loudness
    return jnp.minimum(jnp.maximum(array, -most), most).astype(kind)


def setup_inputs(seed: int = 0) -> dict:
    streams_of = jax.random.split(jax.random.key(seed), 10)
    return {
        "visc_wn": jnp.clip(jnp.exp(math.log(2.0) - 1.3862944 * jax.random.uniform(streams_of[0], (NC, NW, LINES), jnp.float32) ** block_levels(streams_of[0], (NC, NW, LINES), ((1, 2), (2, 16)), -0.2, 0.2)), 0.5, 2.0),
        "conv_wn": jnp.clip(jax.random.uniform(streams_of[1], (NC, NC, NW, LINES), jnp.float32, -0.3, 0.3) * block_levels(streams_of[1], (NC, NC, NW, LINES), ((2, 2), (3, 16)), -0.4, 0.0), -0.3, 0.3),
        "spin": jnp.clip(jax.random.uniform(streams_of[2], (NC, NC, NW, LINES), jnp.float32, -0.3, 0.3) * block_levels(streams_of[2], (NC, NC, NW, LINES), ((2, 2), (3, 16)), -0.4, 0.0), -0.3, 0.3),
        "visc_az": jnp.clip(jnp.exp(math.log(0.015625) - 2.0794415 * jax.random.uniform(streams_of[3], (NC, NW, LINES), jnp.float32) ** block_levels(streams_of[3], (NC, NW, LINES), ((1, 2), (2, 16)), -0.2, 0.2)), 0.001953125, 0.015625),
        "flux_wn": centred(streams_of[4], (NC, NW, LINES), 1.0, 6.0, ((1, 2), (2, 16)), jnp.float32),
        "flux_az": centred(streams_of[5], (NC, NW, LINES), (1.0 / WN_DEV), 0.375, ((1, 2), (2, 16)), jnp.float32),
        "incr_prev": centred(streams_of[6], (NC, NW, LINES), 2.0, 12.0, ((1, 2), (2, 16)), jnp.float32),
        "cell_type": draw_cell_type(jax.random.fold_in(streams_of[9], 71), 0),
        "edge_index": plant(jax.random.randint(streams_of[8], (LINES,), NW // 4, 3 * NW // 4), jax.random.fold_in(streams_of[8], 1), NW // 4, (3 * NW // 4) - 1).astype(jnp.int32),
    }


OUTER_SCALE = 0.25


def block_product(matrix, operand):
    return jnp.sum(matrix[:, :, None] * operand[None], axis=1)


def block_vector(matrix, vector):
    return jnp.sum(matrix * vector[None], axis=1)


def diagonal_of(vector):
    order_size = vector.shape[0]
    identity = jnp.eye(order_size, dtype=vector.dtype).reshape((order_size, order_size) + (1,) * (vector.ndim - 1))
    return identity * vector[None]


def invert(matrix):
    order_size = matrix.shape[0]
    identity = jnp.eye(order_size, dtype=matrix.dtype).reshape((order_size, order_size) + (1,) * (matrix.ndim - 2))
    working = matrix
    result = jnp.broadcast_to(identity, matrix.shape)
    for pivot_row in range(order_size):
        pivot_scale = 1.0 / working[pivot_row, pivot_row]
        row_working = working[pivot_row] * pivot_scale
        row_result = result[pivot_row] * pivot_scale
        column = working[:, pivot_row]
        working = working - column[:, None] * row_working[None]
        result = result - column[:, None] * row_result[None]
        working = working.at[pivot_row].set(row_working)
        result = result.at[pivot_row].set(row_result)
    return result


def reference(visc_wn, conv_wn, spin, visc_az, flux_wn, flux_az, incr_prev, cell_type, edge_index):
    components, points, line_count = visc_wn.shape
    block_lines = S * AZ_DEV
    block_count = line_count // block_lines
    fluid_mask = (cell_type == 0).astype(jnp.float32)
    energy = (jnp.arange(components) == components - 1).astype(jnp.float32)
    keep_mask = jnp.maximum(fluid_mask[None, :], energy[:, None])
    keep_above = jnp.concatenate([keep_mask[:, 1:], jnp.ones((components, 1), jnp.float32)], 1)
    position = jnp.arange(points, dtype=jnp.int32)
    edge_scale = jnp.where(position[:, None] < edge_index[None, :], 1.0, OUTER_SCALE).astype(jnp.float32)
    face_visc = visc_wn * edge_scale[None] * (keep_mask * keep_above)[:, :, None]
    visc_below = jnp.concatenate([jnp.zeros((components, 1, line_count), jnp.float32), face_visc[:, :-1]], 1)
    flux_below = jnp.concatenate([jnp.zeros((components, 1, line_count), jnp.float32), flux_wn[:, :-1]], 1)
    visc_minus = jnp.roll(visc_az, S, axis=2) * keep_mask[:, :, None]
    visc_plus = visc_az * keep_mask[:, :, None]
    azimuthal_diagonal = visc_minus + visc_plus + (1.0 - keep_mask)[:, :, None]
    source = (flux_below - flux_wn + jnp.roll(flux_az, S, axis=2) - flux_az) * keep_mask[:, :, None]
    conv_mask = (keep_mask[:, None] * keep_above[None])[:, :, :, None]
    spin_mask = (keep_mask[:, None] * keep_mask[None])[:, :, :, None]

    def blocks(first_line):
        face_conv = lax.dynamic_slice_in_dim(conv_wn, first_line, block_lines, 3) * conv_mask
        conv_below = jnp.concatenate([jnp.zeros_like(face_conv[:, :, :1]), face_conv[:, :, :-1]], 2)
        twist = lax.dynamic_slice_in_dim(spin, first_line, block_lines, 3) * spin_mask
        visc_here = lax.dynamic_slice_in_dim(face_visc, first_line, block_lines, 2)
        visc_low = lax.dynamic_slice_in_dim(visc_below, first_line, block_lines, 2)
        extra_diag = lax.dynamic_slice_in_dim(azimuthal_diagonal, first_line, block_lines, 2)
        upper_block = (-diagonal_of(visc_here) + face_conv).at[:, :, -1].set(0.0)
        lower_block = -diagonal_of(visc_low) - jnp.swapaxes(conv_below, 0, 1)
        center_block = diagonal_of(visc_low + visc_here + extra_diag) + twist - jnp.swapaxes(twist, 0, 1)
        return lower_block, center_block, upper_block

    def thomas(lower_block, center_block, upper_block, right_side):
        def forward(carry, item):
            couple_prev, value_prev = carry
            low_item, center_item, upper_item, side_item = item
            inverse = invert(center_item - block_product(low_item, couple_prev))
            couple = block_product(inverse, upper_item)
            value_now = block_vector(inverse, side_item - block_vector(low_item, value_prev))
            return (couple, value_now), (couple, value_now)

        start = (jnp.zeros((components, components, block_lines), jnp.float32), jnp.zeros((components, block_lines), jnp.float32))
        items = (jnp.moveaxis(lower_block, 2, 0), jnp.moveaxis(center_block, 2, 0), jnp.moveaxis(upper_block, 2, 0), jnp.moveaxis(right_side, 1, 0))
        _, (couples, values) = lax.scan(forward, start, items)

        def backward(after, item):
            couple, value_now = item
            solved = value_now - block_vector(couple, after)
            return solved, solved

        _, solved_all = lax.scan(backward, jnp.zeros((components, block_lines), jnp.float32), (couples, values), reverse=True)
        return jnp.moveaxis(solved_all, 0, 1)

    def regroup(stacked):
        return jnp.moveaxis(stacked, 0, 2).reshape(components, points, line_count)

    def solve_all(right_side):
        def one_block(block_index):
            first_line = (block_index * block_lines).astype(jnp.int32)
            lower_block, center_block, upper_block = blocks(first_line)
            side_part = lax.dynamic_slice_in_dim(right_side, first_line, block_lines, 2)
            return thomas(lower_block, center_block, upper_block, side_part)

        return regroup(lax.map(one_block, jnp.arange(block_count, dtype=jnp.int32)))

    def offline(vector):
        return visc_minus * jnp.roll(vector, S, axis=2) + visc_plus * jnp.roll(vector, -S, axis=2)

    increment = incr_prev
    for sweep_index in range(SWEEPS):
        increment = solve_all(source + offline(increment))

    def apply_block(block_index):
        first_line = (block_index * block_lines).astype(jnp.int32)
        lower_block, center_block, upper_block = blocks(first_line)
        local_part = lax.dynamic_slice_in_dim(increment, first_line, block_lines, 2)
        below = jnp.concatenate([jnp.zeros_like(local_part[:, :1]), local_part[:, :-1]], 1)
        above = jnp.concatenate([local_part[:, 1:], jnp.zeros_like(local_part[:, :1])], 1)
        return block_vector(center_block, local_part) + block_vector(lower_block, below) + block_vector(upper_block, above)

    applied = regroup(lax.map(apply_block, jnp.arange(block_count, dtype=jnp.int32)))
    defect = (source + offline(increment) - applied) / azimuthal_diagonal
    return increment, defect
```

```python
import jax
import jax.numpy as jnp
from jax import lax
from jax.experimental import pallas as pl
from jax.experimental.pallas import tpu as pltpu
from jax.sharding import PartitionSpec as P

S = 8
SWEEPS = 2
OUTER_SCALE = 0.25
NC = 5
LANES = 128
SUB = 8
NEAR = 2 * S
FAR = 3 * S

CONV, SKEW, VISC, FLUX, EDGE = 0, 25, 35, 40, 45
NEAR_VALUES = 46
VAZ, FAZ, INC = 46, 51, 56
VALUES = 61
NEAR_SLOTS = LANES // NEAR
FAR_SLOTS = LANES // FAR
NEAR_PACKS = -(-NEAR_VALUES // NEAR_SLOTS)
FAR_PACKS = -(-(VALUES - NEAR_VALUES) // FAR_SLOTS)
PACKS = NEAR_PACKS + FAR_PACKS
PAIRS = [(a, b) for a in range(NC) for b in range(a + 1, NC)]


def slot_of(value):
    if value < NEAR_VALUES:
        return value // NEAR_SLOTS, value % NEAR_SLOTS, NEAR
    other = value - NEAR_VALUES
    return NEAR_PACKS + other // FAR_SLOTS, other % FAR_SLOTS, FAR


def tile_reader(visc, conv, spin, vaz, flux, faz, inc, edge):
    def read(value, t, lt):
        rows, lanes = pl.ds(SUB * t, SUB), pl.ds(LANES * lt, LANES)
        if value < SKEW:
            return conv[value, rows, lanes]
        if value < VISC:
            a, b = PAIRS[value - SKEW]
            return spin[a * NC + b, rows, lanes] - spin[b * NC + a, rows, lanes]
        if value == EDGE:
            return jnp.broadcast_to(edge[0:1, lanes].astype(jnp.float32), (SUB, LANES))
        for first, ref in ((VISC, visc), (FLUX, flux), (VAZ, vaz), (FAZ, faz), (INC, inc)):
            if first <= value < first + NC:
                return ref[value - first, rows, lanes]

    return read


def pack_kernel(visc, conv, spin, vaz, flux, faz, inc, edge, even_out, odd_out):
    odd_place = lax.rem(lax.axis_index("az"), 2) == 1
    read = tile_reader(visc, conv, spin, vaz, flux, faz, inc, edge)
    lane = lax.broadcasted_iota(jnp.int32, (SUB, LANES), 1)
    for t in range(2):
        first = [jnp.zeros((SUB, LANES), jnp.float32)] * PACKS
        last = [jnp.zeros((SUB, LANES), jnp.float32)] * PACKS
        for value in range(VALUES):
            pack, slot, width = slot_of(value)
            low = slot * width
            here = (lane >= low) & (lane < low + width)
            low = (LANES - width + slot * width) % LANES
            there = (lane >= low) & (lane < low + width)
            one, two = read(value, t, 0), read(value, t, 1)
            if slot:
                one, two = pltpu.roll(one, slot * width, 1), pltpu.roll(two, slot * width, 1)
            first[pack] = jnp.where(here, one, first[pack])
            last[pack] = jnp.where(there, two, last[pack])
        rows = pl.ds(SUB * t, SUB)
        for pack in range(PACKS):
            even_out[pack, rows, :] = jnp.where(odd_place, first[pack], last[pack])
            odd_out[pack, rows, :] = jnp.where(odd_place, last[pack], first[pack])


def factor(matrix):
    work = [list(row) for row in matrix]
    scale = []
    for p in range(NC):
        scale.append(1.0 / work[p][p])
        for i in range(p + 1, NC):
            work[i][p] = work[i][p] * scale[p]
            for j in range(p + 1, NC):
                work[i][j] = work[i][j] - work[i][p] * work[p][j]
    for p in range(NC):
        work[p][p] = scale[p]
    return work


def substitute(work, side):
    side = list(side)
    for p in range(NC):
        for i in range(p + 1, NC):
            side[i] = side[i] - work[i][p] * side[p]
    for i in reversed(range(NC)):
        for j in range(i + 1, NC):
            side[i] = side[i] - work[i][j] * side[j]
        side[i] = side[i] * work[i][i]
    return side


def dot(row, column):
    terms = [a * b for a, b in zip(row, column)]
    return (terms[0] + terms[1]) + (terms[2] + terms[3]) + terms[4]


def times(matrix, vector):
    return [dot(row, vector) for row in matrix]


def product(left, right):
    columns = [[right[i][j] for i in range(NC)] for j in range(NC)]
    return [[dot(left[i], columns[j]) for j in range(NC)] for i in range(NC)]


def main_kernel(points, *refs):
    (visc, conv, spin, vaz, flux, faz, inc, edge) = refs[0:8]
    sibling = refs[8:15]
    halo_even, halo_odd, sib_even, sib_odd = refs[15:19]
    cell_own, cell_sib = refs[19:21]
    out_inc, out_defect = refs[21:23]
    cells, couple, lower, centre, upper, lu, sides, solved, vmin, vplus, azd, src, out_cells = refs[23:]

    core = lax.axis_index("wn")
    odd_place = lax.rem(lax.axis_index("az"), 2)
    row = lax.broadcasted_iota(jnp.int32, (SUB, LANES), 0)
    lane = lax.broadcasted_iota(jnp.int32, (SUB, LANES), 1)
    is_a = lax.rem(row, 2) == 0

    def put(value, t, place, chain, tile):
        start = pl.multiple_of(SUB * (2 * place + chain), SUB)
        cells[2 * value + (t + chain) % 2 if isinstance(chain, int) else 2 * value + jnp.bitwise_xor(t, chain),
              pl.ds(start, SUB), :] = tile

    for chain, arrays, halos in (
        (core, (visc, conv, spin, vaz, flux, faz, inc), (halo_even, halo_odd)),
        (1 - core, sibling, (sib_even, sib_odd)),
    ):
        read = tile_reader(*arrays, edge)
        sign = jnp.where(chain == 0, 1.0, -1.0).astype(jnp.float32)
        for value in range(VALUES):
            pack, slot, width = slot_of(value)
            for t in range(2):
                tiles = [(0, read(value, t, 0)), (1, read(value, t, 1))]
                for halo, place in ((halos[0], 2 + odd_place), (halos[1], 3 - odd_place)):
                    tile = halo[pack, pl.ds(SUB * t, SUB), :]
                    if slot:
                        tile = pltpu.roll(tile, LANES - slot * width, 1)
                    tiles.append((place, tile))
                for place, tile in tiles:
                    put(value, t, place, chain, tile * sign if value < SKEW else tile)

    def at(value, k):
        return cells[2 * value + k // SUB, pl.ds(k % SUB, SUB, stride=SUB), :]

    def bt(value, k):
        return cells[2 * value + k // SUB, pl.ds(SUB - 1 - k % SUB, SUB, stride=SUB), :]

    def both(value, ka, kb, other=None):
        return jnp.where(is_a, at(value, ka), bt(value if other is None else other, kb))

    def before(x):
        y = pltpu.roll(x, S, 1)
        return jnp.where(lane < S, pltpu.roll(y, 2, 0), y)

    def after(x):
        y = pltpu.roll(x, LANES - S, 1)
        return jnp.where(lane >= LANES - S, pltpu.roll(y, SUB - 2, 0), y)

    def swap(x):
        return jnp.where(is_a, pltpu.roll(x, SUB - 1, 0), pltpu.roll(x, 1, 0))

    edges = cells[2 * EDGE, pl.ds(0, SUB, stride=SUB), :]

    def fluid(k):
        if k >= points:
            return jnp.ones((SUB, LANES), jnp.float32)
        kind = jnp.where(core == 0, cell_own[k], cell_sib[k])
        return jnp.where(is_a, jnp.where(kind == 0, 1.0, 0.0).astype(jnp.float32), 1.0)

    def edge_scale(face_a, face_b):
        face = jnp.where(is_a, float(face_a), float(face_b))
        return jnp.where(face < edges, 1.0, OUTER_SCALE)

    one = jnp.ones((SUB, LANES), jnp.float32)
    zero = jnp.zeros((SUB, LANES), jnp.float32)
    total = 2 * points
    last = points - 1
    previous = None
    for k in range(points):
        keep = [fluid(k)] * (NC - 1) + [one]
        keep_above = [fluid(k + 1)] * (NC - 1) + [one]
        if k < last:
            conv_out = [[both(a * NC + b, k, k + 1, b * NC + a) for b in range(NC)] for a in range(NC)]
            visc_out = [both(VISC + c, k, k + 1) for c in range(NC)]
        else:
            face = [[at(a * NC + b, k) for b in range(NC)] for a in range(NC)]
            conv_out = [[jnp.where(is_a, face[a][b], -pltpu.roll(face[b][a], 1, 0)) for b in range(NC)] for a in range(NC)]
            raw = [at(VISC + c, k) for c in range(NC)]
            visc_out = [jnp.where(is_a, raw[c], pltpu.roll(raw[c], 1, 0)) for c in range(NC)]
        conv_out = [[conv_out[a][b] * (keep[a] * keep_above[b]) for b in range(NC)] for a in range(NC)]
        scale = edge_scale(k, total - 2 - k)
        visc_out = [visc_out[c] * scale * (keep[c] * keep_above[c]) for c in range(NC)]
        if k == 0:
            scale = edge_scale(0, total - 1)
            visc_in = [jnp.where(is_a, 0.0, bt(VISC + c, 0) * scale) for c in range(NC)]

        vm, vp, az_diag, source, side = [], [], [], [], []
        for c in range(NC):
            here = both(VAZ + c, k, k)
            vm.append(before(here) * keep[c])
            vp.append(here * keep[c])
            az_diag.append(vm[c] + vp[c] + (1.0 - keep[c]))
            flux_here = both(FLUX + c, k, k)
            if k == 0:
                flux_below = jnp.where(is_a, 0.0, bt(FLUX + c, 1))
            elif k < last:
                flux_below = both(FLUX + c, k - 1, k + 1)
            else:
                flux_below = jnp.where(is_a, at(FLUX + c, k - 1), pltpu.roll(at(FLUX + c, k), 1, 0))
            flux_side = both(FAZ + c, k, k)
            source.append((flux_below - flux_here + before(flux_side) - flux_side) * keep[c])
            start = both(INC + c, k, k)
            side.append(source[c] + (vm[c] * before(start) + vp[c] * after(start)))
            vmin[k * NC + c], vplus[k * NC + c] = vm[c], vp[c]
            azd[k * NC + c], src[k * NC + c] = az_diag[c], source[c]

        matrix = [[None] * NC for _ in range(NC)]
        for c in range(NC):
            matrix[c][c] = visc_in[c] + visc_out[c] + az_diag[c]
        for n, (a, b) in enumerate(PAIRS):
            skew = both(SKEW + n, k, k) * (keep[a] * keep[b])
            matrix[a][b], matrix[b][a] = skew, -skew
        up = [[conv_out[a][b] - visc_out[a] if a == b else conv_out[a][b] for b in range(NC)] for a in range(NC)]
        for a in range(NC):
            for b in range(NC):
                centre[k * 25 + a * NC + b] = matrix[a][b]
                upper[k * 25 + a * NC + b] = up[a][b]
        if previous is not None:
            conv_in, couple_in, y_in = previous
            low = [[-visc_in[a] - conv_in[a][a] if a == b else -conv_in[b][a] for b in range(NC)] for a in range(NC)]
            for a in range(NC):
                for b in range(NC):
                    lower[k * 25 + a * NC + b] = low[a][b]
            moved = product(low, couple_in)
            matrix = [[matrix[a][b] - moved[a][b] for b in range(NC)] for a in range(NC)]
            shift = times(low, y_in)
            side = [side[c] - shift[c] for c in range(NC)]
        work = factor(matrix)
        columns = [substitute(work, [up[i][j] for i in range(NC)]) for j in range(NC)]
        couple_now = [[columns[j][i] for j in range(NC)] for i in range(NC)]
        y = substitute(work, side)
        for a in range(NC):
            sides[k * NC + a] = y[a]
            for b in range(NC):
                lu[k * 25 + a * NC + b] = work[a][b]
                couple[k * 25 + a * NC + b] = couple_now[a][b]
        previous = (conv_out, couple_now, y)
        visc_in = visc_out

    def block(ref, k):
        return [[ref[k * 25 + a * NC + b] for b in range(NC)] for a in range(NC)]

    def vector(ref, k):
        return [ref[k * NC + c] for c in range(NC)]

    couple_end = couple_now
    crossed = product(couple_end, [[swap(couple_end[a][b]) for b in range(NC)] for a in range(NC)])
    meeting = factor([[(1.0 if a == b else 0.0) - crossed[a][b] for b in range(NC)] for a in range(NC)])

    def finish(y):
        shift = times(couple_end, [swap(v) for v in y])
        x = substitute(meeting, [y[c] - shift[c] for c in range(NC)])
        for c in range(NC):
            solved[last * NC + c] = x[c]
        for k in reversed(range(last)):
            shift = times(block(couple, k), x)
            y_here = vector(sides, k)
            x = [y_here[c] - shift[c] for c in range(NC)]
            for c in range(NC):
                solved[k * NC + c] = x[c]

    finish(y)
    for sweep in range(1, SWEEPS):
        for k in range(points):
            source, vm, vp, x = vector(src, k), vector(vmin, k), vector(vplus, k), vector(solved, k)
            side = [source[c] + (vm[c] * before(x[c]) + vp[c] * after(x[c])) for c in range(NC)]
            if k:
                shift = times(block(lower, k), y)
                side = [side[c] - shift[c] for c in range(NC)]
            y = substitute(block(lu, k), side)
            for c in range(NC):
                sides[k * NC + c] = y[c]
        finish(y)

    for k in range(points):
        source, vm, vp, x = vector(src, k), vector(vmin, k), vector(vplus, k), vector(solved, k)
        diag = vector(azd, k)
        beyond = vector(solved, k + 1) if k < last else [swap(v) for v in x]
        inner = times(block(centre, k), x)
        outer = times(block(upper, k), beyond)
        under = times(block(lower, k), vector(solved, k - 1)) if k else [zero] * NC
        place = jnp.where(core == 0, k % SUB, SUB - 1 - k % SUB)
        t = jnp.where(core == 0, k // SUB, 1 - k // SUB)
        for c in range(NC):
            offline = vm[c] * before(x[c]) + vp[c] * after(x[c])
            defect = (source[c] + offline - (inner[c] + under[c] + outer[c])) / diag[c]
            out_cells[2 * c + t, pl.ds(place, SUB, stride=SUB), :] = x[c]
            out_cells[2 * (NC + c) + t, pl.ds(place, SUB, stride=SUB), :] = defect
    for c in range(NC):
        for t in range(2):
            for lt in range(2):
                start = pl.multiple_of(SUB * (2 * lt + core), SUB)
                rows, lanes = pl.ds(SUB * t, SUB), pl.ds(LANES * lt, LANES)
                out_inc[c, rows, lanes] = out_cells[2 * c + t, pl.ds(start, SUB), :]
                out_defect[c, rows, lanes] = out_cells[2 * (NC + c) + t, pl.ds(start, SUB), :]


def per_device(visc_wn, conv_wn, spin, visc_az, flux_wn, flux_az, incr_prev, cell_type, edge_index):
    components, points, line_count = visc_wn.shape
    assert components == NC and points == 2 * SUB and line_count == 2 * LANES
    count = lax.axis_size("az")
    assert count % 2 == 0
    even_pairs = [(a, a ^ 1) for a in range(count)]
    odd_pairs = [(a, (a + 1 if a % 2 else a - 1) % count) for a in range(count)]
    vmem, smem = pl.BlockSpec(memory_space=pltpu.VMEM), pl.BlockSpec(memory_space=pltpu.SMEM)

    blocks = (NC * NC, points, line_count)
    own = (visc_wn, conv_wn.reshape(blocks), spin.reshape(blocks), visc_az, flux_wn, flux_az, incr_prev)
    edge = edge_index.reshape(1, line_count)
    pack = jax.ShapeDtypeStruct((PACKS, points, LANES), jnp.float32)
    even, odd = pl.pallas_call(
        pack_kernel,
        out_shape=(pack, pack),
        in_specs=[vmem] * 8,
        out_specs=(vmem, vmem),
        name="pack_halo",
        compiler_params=pltpu.CompilerParams(vmem_limit_bytes=32 << 20),
    )(*own, edge)
    halo_even = lax.ppermute(even, "az", even_pairs)
    halo_odd = lax.ppermute(odd, "az", odd_pairs)

    def cross(array):
        return lax.ppermute(array, "wn", [(0, 1), (1, 0)])

    sibling = tuple(cross(array) for array in own)
    cell_sib = cross(cell_type)
    sib_even, sib_odd = cross(halo_even), cross(halo_odd)

    step = pltpu.VMEM((points * NC * NC, SUB, LANES), jnp.float32)
    line = pltpu.VMEM((points * NC, SUB, LANES), jnp.float32)
    out = jax.ShapeDtypeStruct((NC, points, line_count), jnp.float32)
    return pl.pallas_call(
        lambda *refs: main_kernel(points, *refs),
        out_shape=(out, out),
        in_specs=[vmem] * 19 + [smem] * 2,
        out_specs=(vmem, vmem),
        scratch_shapes=[pltpu.VMEM((2 * VALUES, SUB * SUB, LANES), jnp.float32)]
        + [step] * 5
        + [line] * 6
        + [pltpu.VMEM((4 * NC, SUB * SUB, LANES), jnp.float32)],
        name="relax_lines",
        compiler_params=pltpu.CompilerParams(vmem_limit_bytes=40 << 20),
    )(*own, edge, *sibling, halo_even, halo_odd, sib_even, sib_odd, cell_type, cell_sib)


def solution(mesh):
    in_specs = (
        P(None, "wn", "az"),
        P(None, None, "wn", "az"),
        P(None, None, "wn", "az"),
        P(None, "wn", "az"),
        P(None, "wn", "az"),
        P(None, "wn", "az"),
        P(None, "wn", "az"),
        P("wn"),
        P("az"),
    )
    out_specs = (P(None, "wn", "az"), P(None, "wn", "az"))
    return jax.shard_map(
        per_device, mesh=mesh, in_specs=in_specs, out_specs=out_specs, check_vma=False
    )
```

```python
import jax
import jax.numpy as jnp
from jax import lax
from jax.experimental import pallas as pl
from jax.experimental.pallas import tpu as pltpu
from jax.sharding import PartitionSpec as P

S = 8
SWEEPS = 2
OUTER_SCALE = 0.25
NC = 5
LANES = 128
SUB = 8
NEAR = 2 * S
FAR = 3 * S

CONV, SKEW, VISC, FLUX, EDGE, FLUID = 0, 25, 35, 40, 45, 46
NEAR_VALUES = 47
VAZ, FAZ, INC = 47, 52, 57
VALUES = 62
SOLID_MOST = 4
NEAR_SLOTS = LANES // NEAR
FAR_SLOTS = LANES // FAR
NEAR_PACKS = -(-NEAR_VALUES // NEAR_SLOTS)
FAR_PACKS = -(-(VALUES - NEAR_VALUES) // FAR_SLOTS)
PACKS = NEAR_PACKS + FAR_PACKS
PAIRS = [(a, b) for a in range(NC) for b in range(a + 1, NC)]


def slot_of(value):
    if value < NEAR_VALUES:
        return value // NEAR_SLOTS, value % NEAR_SLOTS, NEAR
    other = value - NEAR_VALUES
    return NEAR_PACKS + other // FAR_SLOTS, other % FAR_SLOTS, FAR


def tile_reader(conv, spin, edge, lines):
    def read(value, t, lt):
        rows, lanes = pl.ds(SUB * t, SUB), pl.ds(LANES * lt, LANES)
        if value < SKEW:
            return conv[value, rows, lanes]
        if value < VISC:
            a, b = PAIRS[value - SKEW]
            return spin[a * NC + b, rows, lanes] - spin[b * NC + a, rows, lanes]
        if value == EDGE:
            return jnp.broadcast_to(edge[0:1, lanes].astype(jnp.float32), (SUB, LANES))
        for first, ref in zip((VISC, FLUX, VAZ, FAZ, INC), lines):
            if first <= value < first + NC:
                return ref[value - first, rows, lanes]

    return read


def lines_of(ref):
    return [ref.at[pl.ds(NC * n, NC)] for n in range(5)]


def pack_kernel(conv_hbm, spin_hbm, edge_hbm, visc_hbm, flux_hbm, vaz_hbm, faz_hbm, inc_hbm, cells_hbm,
                even_out, odd_out, stack_out, conv, spin, edge, stack, cells, sems, stack_sem):
    odd_place = lax.rem(lax.axis_index("az"), 2) == 1
    copies = []
    for n, ref in enumerate((visc_hbm, flux_hbm, vaz_hbm, faz_hbm, inc_hbm)):
        copies.append(pltpu.make_async_copy(ref, stack.at[pl.ds(NC * n, NC)], sems.at[n]))
    copies.append(pltpu.make_async_copy(edge_hbm, edge, sems.at[5]))
    for n in range(NC):
        part = pl.ds(NC * n, NC)
        copies.append(pltpu.make_async_copy(conv_hbm.at[part], conv.at[part], sems.at[6 + n]))
        copies.append(pltpu.make_async_copy(spin_hbm.at[part], spin.at[part], sems.at[11 + n]))
    copies.append(pltpu.make_async_copy(cells_hbm, cells, sems.at[16]))
    for copy in copies:
        copy.start()
    for copy in copies[:5]:
        copy.wait()
    stacked = pltpu.make_async_copy(stack, stack_out, stack_sem)
    stacked.start()
    for copy in copies[5:]:
        copy.wait()
    read = tile_reader(conv, spin, edge, lines_of(stack))
    lane = lax.broadcasted_iota(jnp.int32, (SUB, LANES), 1)
    row = lax.broadcasted_iota(jnp.int32, (SUB, LANES), 0)
    for t in range(2):
        fluid = jnp.ones((SUB, LANES), jnp.float32)
        for p in range(SOLID_MOST if t == 0 else 0):
            fluid = jnp.where(row == p, jnp.where(cells[p] == 0, 1.0, 0.0).astype(jnp.float32), fluid)
        first = [jnp.zeros((SUB, LANES), jnp.float32)] * PACKS
        last = [jnp.zeros((SUB, LANES), jnp.float32)] * PACKS
        for value in range(VALUES):
            pack, slot, width = slot_of(value)
            low = slot * width
            here = (lane >= low) & (lane < low + width)
            low = (LANES - width + slot * width) % LANES
            there = (lane >= low) & (lane < low + width)
            if value == FLUID:
                one, two = fluid, fluid
            else:
                one, two = read(value, t, 0), read(value, t, 1)
                if slot:
                    one, two = pltpu.roll(one, slot * width, 1), pltpu.roll(two, slot * width, 1)
            first[pack] = jnp.where(here, one, first[pack])
            last[pack] = jnp.where(there, two, last[pack])
        rows = pl.ds(SUB * t, SUB)
        for pack in range(PACKS):
            even_out[pack, rows, :] = jnp.where(odd_place, first[pack], last[pack])
            odd_out[pack, rows, :] = jnp.where(odd_place, last[pack], first[pack])
    stacked.wait()


def factor(matrix):
    work = [list(row) for row in matrix]
    scale = []
    for p in range(NC):
        scale.append(1.0 / work[p][p])
        for i in range(p + 1, NC):
            work[i][p] = work[i][p] * scale[p]
            for j in range(p + 1, NC):
                work[i][j] = work[i][j] - work[i][p] * work[p][j]
    for p in range(NC):
        work[p][p] = scale[p]
    return work


def substitute(work, side):
    side = list(side)
    for p in range(NC):
        for i in range(p + 1, NC):
            side[i] = side[i] - work[i][p] * side[p]
    for i in reversed(range(NC)):
        for j in range(i + 1, NC):
            side[i] = side[i] - work[i][j] * side[j]
        side[i] = side[i] * work[i][i]
    return side


def dot(row, column):
    terms = [a * b for a, b in zip(row, column)]
    return (terms[0] + terms[1]) + (terms[2] + terms[3]) + terms[4]


def times(matrix, vector):
    return [dot(row, vector) for row in matrix]


def product(left, right):
    columns = [[right[i][j] for i in range(NC)] for j in range(NC)]
    return [[dot(left[i], columns[j]) for j in range(NC)] for i in range(NC)]


def main_kernel(points, *refs):
    conv, spin, edge, *lines = refs[0:8]
    sib_conv, sib_spin, sib_stack = refs[8:11]
    halo_even, halo_odd, sib_even, sib_odd = refs[11:15]
    out_inc, out_defect = refs[15:17]
    cells, couple, lower, centre, upper, lu, sides, solved, vmin, vplus, azd, src, out_cells = refs[17:]

    core = lax.axis_index("wn")
    odd_place = lax.rem(lax.axis_index("az"), 2)
    row = lax.broadcasted_iota(jnp.int32, (SUB, LANES), 0)
    lane = lax.broadcasted_iota(jnp.int32, (SUB, LANES), 1)
    is_a = lax.rem(row, 2) == 0

    def put(value, t, place, chain, tile):
        start = pl.multiple_of(SUB * (2 * place + chain), SUB)
        cells[2 * value + jnp.bitwise_xor(t, chain), pl.ds(start, SUB), :] = tile

    for chain, arrays, halos in (
        (core, (conv, spin, edge, lines), (halo_even, halo_odd)),
        (1 - core, (sib_conv, sib_spin, edge, lines_of(sib_stack)), (sib_even, sib_odd)),
    ):
        read = tile_reader(*arrays)
        sign = jnp.where(chain == 0, 1.0, -1.0).astype(jnp.float32)
        for value in range(VALUES):
            if value == FLUID:
                continue
            pack, slot, width = slot_of(value)
            for t in range(2):
                tiles = [(0, read(value, t, 0)), (1, read(value, t, 1))]
                for halo, place in ((halos[0], 2 + odd_place), (halos[1], 3 - odd_place)):
                    tile = halo[pack, pl.ds(SUB * t, SUB), :]
                    if slot:
                        tile = pltpu.roll(tile, LANES - slot * width, 1)
                    tiles.append((place, tile))
                for place, tile in tiles:
                    put(value, t, place, chain, tile * sign if value < SKEW else tile)

    def at(value, k):
        return cells[2 * value + k // SUB, pl.ds(k % SUB, SUB, stride=SUB), :]

    def bt(value, k):
        return cells[2 * value + k // SUB, pl.ds(SUB - 1 - k % SUB, SUB, stride=SUB), :]

    def both(value, ka, kb, other=None):
        return jnp.where(is_a, at(value, ka), bt(value if other is None else other, kb))

    def before(x):
        y = pltpu.roll(x, S, 1)
        return jnp.where(lane < S, pltpu.roll(y, 2, 0), y)

    def after(x):
        y = pltpu.roll(x, LANES - S, 1)
        return jnp.where(lane >= LANES - S, pltpu.roll(y, SUB - 2, 0), y)

    def swap(x):
        return jnp.where(is_a, pltpu.roll(x, SUB - 1, 0), pltpu.roll(x, 1, 0))

    edges = cells[2 * EDGE, pl.ds(0, SUB, stride=SUB), :]

    fluid_pack, fluid_slot, fluid_width = slot_of(FLUID)
    fluid_tile = jnp.where(core == 0, halo_even[fluid_pack, 0:SUB, :], sib_even[fluid_pack, 0:SUB, :])
    fluid_lane = jnp.where(odd_place == 0, fluid_slot * fluid_width, (fluid_slot - 1) * fluid_width)
    fluid_tile = jnp.max(jnp.where(lane == fluid_lane, fluid_tile, 0.0), axis=1, keepdims=True)

    def fluid(k):
        return jnp.where(is_a, jnp.broadcast_to(fluid_tile[k : k + 1, :], (SUB, LANES)), 1.0)

    def edge_scale(face_a, face_b):
        face = jnp.where(is_a, float(face_a), float(face_b))
        return jnp.where(face < edges, 1.0, OUTER_SCALE)

    one = jnp.ones((SUB, LANES), jnp.float32)
    zero = jnp.zeros((SUB, LANES), jnp.float32)
    total = 2 * points
    last = points - 1
    previous = None
    for k in range(points):
        solid = k < SOLID_MOST
        if solid:
            keep = [fluid(k)] * (NC - 1) + [one]
            keep_above = [fluid(k + 1) if k + 1 < SOLID_MOST else one] * (NC - 1) + [one]
        if k < last:
            conv_out = [[both(a * NC + b, k, k + 1, b * NC + a) for b in range(NC)] for a in range(NC)]
            visc_out = [both(VISC + c, k, k + 1) for c in range(NC)]
        else:
            face = [[at(a * NC + b, k) for b in range(NC)] for a in range(NC)]
            conv_out = [[jnp.where(is_a, face[a][b], -pltpu.roll(face[b][a], 1, 0)) for b in range(NC)] for a in range(NC)]
            raw = [at(VISC + c, k) for c in range(NC)]
            visc_out = [jnp.where(is_a, raw[c], pltpu.roll(raw[c], 1, 0)) for c in range(NC)]
        scale = edge_scale(k, total - 2 - k)
        visc_out = [visc_out[c] * scale for c in range(NC)]
        if solid:
            conv_out = [[conv_out[a][b] * (keep[a] * keep_above[b]) for b in range(NC)] for a in range(NC)]
            visc_out = [visc_out[c] * (keep[c] * keep_above[c]) for c in range(NC)]
        if k == 0:
            scale = edge_scale(0, total - 1)
            visc_in = [jnp.where(is_a, 0.0, bt(VISC + c, 0) * scale) for c in range(NC)]

        vm, vp, az_diag, source, side = [], [], [], [], []
        for c in range(NC):
            here = both(VAZ + c, k, k)
            vm.append(before(here) * keep[c] if solid else before(here))
            vp.append(here * keep[c] if solid else here)
            az_diag.append(vm[c] + vp[c] + (1.0 - keep[c]) if solid else vm[c] + vp[c])
            flux_here = both(FLUX + c, k, k)
            if k == 0:
                flux_below = jnp.where(is_a, 0.0, bt(FLUX + c, 1))
            elif k < last:
                flux_below = both(FLUX + c, k - 1, k + 1)
            else:
                flux_below = jnp.where(is_a, at(FLUX + c, k - 1), pltpu.roll(at(FLUX + c, k), 1, 0))
            flux_side = both(FAZ + c, k, k)
            flow = flux_below - flux_here + before(flux_side) - flux_side
            source.append(flow * keep[c] if solid else flow)
            start = both(INC + c, k, k)
            side.append(source[c] + (vm[c] * before(start) + vp[c] * after(start)))
            vmin[k * NC + c], vplus[k * NC + c] = vm[c], vp[c]
            azd[k * NC + c], src[k * NC + c] = az_diag[c], source[c]

        matrix = [[None] * NC for _ in range(NC)]
        for c in range(NC):
            matrix[c][c] = visc_in[c] + visc_out[c] + az_diag[c]
        for n, (a, b) in enumerate(PAIRS):
            skew = both(SKEW + n, k, k)
            if solid:
                skew = skew * (keep[a] * keep[b])
            matrix[a][b], matrix[b][a] = skew, -skew
        up = [[conv_out[a][b] - visc_out[a] if a == b else conv_out[a][b] for b in range(NC)] for a in range(NC)]
        for a in range(NC):
            for b in range(NC):
                centre[k * 25 + a * NC + b] = matrix[a][b]
                upper[k * 25 + a * NC + b] = up[a][b]
        if previous is not None:
            conv_in, couple_in, y_in = previous
            low = [[-visc_in[a] - conv_in[a][a] if a == b else -conv_in[b][a] for b in range(NC)] for a in range(NC)]
            for a in range(NC):
                for b in range(NC):
                    lower[k * 25 + a * NC + b] = low[a][b]
            moved = product(low, couple_in)
            matrix = [[matrix[a][b] - moved[a][b] for b in range(NC)] for a in range(NC)]
            shift = times(low, y_in)
            side = [side[c] - shift[c] for c in range(NC)]
        work = factor(matrix)
        columns = [substitute(work, [up[i][j] for i in range(NC)]) for j in range(NC)]
        couple_now = [[columns[j][i] for j in range(NC)] for i in range(NC)]
        y = substitute(work, side)
        for a in range(NC):
            sides[k * NC + a] = y[a]
            for b in range(NC):
                lu[k * 25 + a * NC + b] = work[a][b]
                couple[k * 25 + a * NC + b] = couple_now[a][b]
        previous = (conv_out, couple_now, y)
        visc_in = visc_out

    def block(ref, k):
        return [[ref[k * 25 + a * NC + b] for b in range(NC)] for a in range(NC)]

    def vector(ref, k):
        return [ref[k * NC + c] for c in range(NC)]

    couple_end = couple_now
    crossed = product(couple_end, [[swap(couple_end[a][b]) for b in range(NC)] for a in range(NC)])
    meeting = factor([[(1.0 if a == b else 0.0) - crossed[a][b] for b in range(NC)] for a in range(NC)])

    def finish(y):
        shift = times(couple_end, [swap(v) for v in y])
        x = substitute(meeting, [y[c] - shift[c] for c in range(NC)])
        for c in range(NC):
            solved[last * NC + c] = x[c]
        for k in reversed(range(last)):
            shift = times(block(couple, k), x)
            y_here = vector(sides, k)
            x = [y_here[c] - shift[c] for c in range(NC)]
            for c in range(NC):
                solved[k * NC + c] = x[c]

    finish(y)
    for sweep in range(1, SWEEPS):
        for k in range(points):
            source, vm, vp, x = vector(src, k), vector(vmin, k), vector(vplus, k), vector(solved, k)
            side = [source[c] + (vm[c] * before(x[c]) + vp[c] * after(x[c])) for c in range(NC)]
            if k:
                shift = times(block(lower, k), y)
                side = [side[c] - shift[c] for c in range(NC)]
            y = substitute(block(lu, k), side)
            for c in range(NC):
                sides[k * NC + c] = y[c]
        finish(y)

    for k in range(points):
        source, vm, vp, x = vector(src, k), vector(vmin, k), vector(vplus, k), vector(solved, k)
        diag = vector(azd, k)
        beyond = vector(solved, k + 1) if k < last else [swap(v) for v in x]
        inner = times(block(centre, k), x)
        outer = times(block(upper, k), beyond)
        under = times(block(lower, k), vector(solved, k - 1)) if k else [zero] * NC
        place = jnp.where(core == 0, k % SUB, SUB - 1 - k % SUB)
        t = jnp.where(core == 0, k // SUB, 1 - k // SUB)
        for c in range(NC):
            offline = vm[c] * before(x[c]) + vp[c] * after(x[c])
            defect = (source[c] + offline - (inner[c] + under[c] + outer[c])) / diag[c]
            out_cells[2 * c + t, pl.ds(place, SUB, stride=SUB), :] = x[c]
            out_cells[2 * (NC + c) + t, pl.ds(place, SUB, stride=SUB), :] = defect
    for c in range(NC):
        for t in range(2):
            for lt in range(2):
                start = pl.multiple_of(SUB * (2 * lt + core), SUB)
                rows, lanes = pl.ds(SUB * t, SUB), pl.ds(LANES * lt, LANES)
                out_inc[c, rows, lanes] = out_cells[2 * c + t, pl.ds(start, SUB), :]
                out_defect[c, rows, lanes] = out_cells[2 * (NC + c) + t, pl.ds(start, SUB), :]


def per_device(visc_wn, conv_wn, spin, visc_az, flux_wn, flux_az, incr_prev, cell_type, edge_index):
    components, points, line_count = visc_wn.shape
    assert components == NC and points == 2 * SUB and line_count == 2 * LANES
    count = lax.axis_size("az")
    assert count % 2 == 0
    even_pairs = [(a, a ^ 1) for a in range(count)]
    odd_pairs = [(a, (a + 1 if a % 2 else a - 1) % count) for a in range(count)]
    vmem, hbm = (pl.BlockSpec(memory_space=m) for m in (pltpu.VMEM, pltpu.HBM))

    blocks = (NC * NC, points, line_count)
    conv, spin = conv_wn.reshape(blocks), spin.reshape(blocks)
    edge = edge_index.reshape(1, line_count)
    lines = (visc_wn, flux_wn, visc_az, flux_az, incr_prev)
    pack = jax.ShapeDtypeStruct((PACKS, points, LANES), jnp.float32)
    block_array = pltpu.VMEM(blocks, jnp.float32)
    even, odd, stack = pl.pallas_call(
        pack_kernel,
        out_shape=(pack, pack, jax.ShapeDtypeStruct(blocks, jnp.float32)),
        in_specs=[hbm] * 9,
        out_specs=(vmem, vmem, hbm),
        scratch_shapes=[
            block_array,
            block_array,
            pltpu.VMEM((1, line_count), jnp.int32),
            block_array,
            pltpu.SMEM((points,), jnp.int32),
            pltpu.SemaphoreType.DMA((17,)),
            pltpu.SemaphoreType.DMA,
        ],
        name="pack_halo",
        compiler_params=pltpu.CompilerParams(vmem_limit_bytes=32 << 20),
    )(*(pltpu.with_memory_space_constraint(array, pltpu.HBM) for array in (conv, spin, edge, *lines, cell_type)))
    even, odd, *late = lax.optimization_barrier((even, odd, conv, spin, stack))
    halo_even = lax.ppermute(even, "az", even_pairs)
    halo_odd = lax.ppermute(odd, "az", odd_pairs)

    def cross(array):
        return lax.ppermute(array, "wn", [(0, 1), (1, 0)])

    sibling = tuple(cross(array) for array in late)
    sib_even, sib_odd = cross(halo_even), cross(halo_odd)

    step = pltpu.VMEM((points * NC * NC, SUB, LANES), jnp.float32)
    line = pltpu.VMEM((points * NC, SUB, LANES), jnp.float32)
    out = jax.ShapeDtypeStruct((NC, points, line_count), jnp.float32)
    return pl.pallas_call(
        lambda *refs: main_kernel(points, *refs),
        out_shape=(out, out),
        in_specs=[vmem] * 15,
        out_specs=(vmem, vmem),
        scratch_shapes=[pltpu.VMEM((2 * VALUES, SUB * SUB, LANES), jnp.float32)]
        + [step] * 5
        + [line] * 6
        + [pltpu.VMEM((4 * NC, SUB * SUB, LANES), jnp.float32)],
        name="relax_lines",
        compiler_params=pltpu.CompilerParams(vmem_limit_bytes=40 << 20),
    )(conv, spin, edge, *lines, *sibling, halo_even, halo_odd, sib_even, sib_odd)


def solution(mesh):
    in_specs = (
        P(None, "wn", "az"),
        P(None, None, "wn", "az"),
        P(None, None, "wn", "az"),
        P(None, "wn", "az"),
        P(None, "wn", "az"),
        P(None, "wn", "az"),
        P(None, "wn", "az"),
        P("wn"),
        P("az"),
    )
    out_specs = (P(None, "wn", "az"), P(None, "wn", "az"))
    return jax.shard_map(
        per_device, mesh=mesh, in_specs=in_specs, out_specs=out_specs, check_vma=False
    )
```

```python
import jax
import jax.numpy as jnp
from jax import lax
from jax.experimental import pallas as pl
from jax.experimental.pallas import tpu as pltpu
from jax.sharding import PartitionSpec as P

S = 8
SWEEPS = 2
OUTER_SCALE = 0.25
NC = 5
LANES = 128
SUB = 8
NEAR = 2 * S
FAR = 3 * S

CONV, SKEW, VISC, FLUX, EDGE, FLUID = 0, 25, 35, 40, 45, 46
NEAR_VALUES = 47
VAZ, FAZ, INC = 47, 52, 57
VALUES = 62
BELOW, STORED = 62, 67
SLOTS = 18
SOLID_MOST = 4
NEAR_SLOTS = LANES // NEAR
FAR_SLOTS = LANES // FAR
NEAR_PACKS = -(-NEAR_VALUES // NEAR_SLOTS)
FAR_PACKS = -(-(VALUES - NEAR_VALUES) // FAR_SLOTS)
PACKS = NEAR_PACKS + FAR_PACKS
PAIRS = [(a, b) for a in range(NC) for b in range(a + 1, NC)]


def slot_of(value):
    if value < NEAR_VALUES:
        return value // NEAR_SLOTS, value % NEAR_SLOTS, NEAR
    other = value - NEAR_VALUES
    return NEAR_PACKS + other // FAR_SLOTS, other % FAR_SLOTS, FAR


def tile_reader(conv, spin, edge, lines):
    def read(value, t, lt):
        rows, lanes = pl.ds(SUB * t, SUB), pl.ds(LANES * lt, LANES)
        if value < SKEW:
            return conv[value, rows, lanes]
        if value < VISC:
            a, b = PAIRS[value - SKEW]
            return spin[a * NC + b, rows, lanes] - spin[b * NC + a, rows, lanes]
        if value == EDGE:
            return jnp.broadcast_to(edge[0:1, lanes].astype(jnp.float32), (SUB, LANES))
        for first, ref in zip((VISC, FLUX, VAZ, FAZ, INC), lines):
            if first <= value < first + NC:
                return ref[value - first, rows, lanes]

    return read


def parts_of(ref):
    lines = [ref.at[pl.ds(2 * NC * NC + NC * n, NC)] for n in range(5)]
    return ref.at[pl.ds(0, NC * NC)], ref.at[pl.ds(NC * NC, NC * NC)], lines


def mirror(tile, chain):
    row = lax.broadcasted_iota(jnp.int32, (SUB, LANES), 0)
    return jnp.take_along_axis(tile, jnp.where(chain == 0, row, SUB - 1 - row), axis=0)


def pack_kernel(conv_hbm, spin_hbm, edge_hbm, visc_hbm, flux_hbm, vaz_hbm, faz_hbm, inc_hbm, cells_hbm,
                even_out, odd_out, bulk, edge, cells, sems):
    odd_place = lax.rem(lax.axis_index("az"), 2) == 1
    core = lax.axis_index("wn")
    conv, spin, lines = parts_of(bulk)
    copies = []
    for n in range(NC):
        part = pl.ds(NC * n, NC)
        copies.append(pltpu.make_async_copy(conv_hbm.at[part], conv.at[part], sems.at[n]))
    for n, ref in enumerate((visc_hbm, flux_hbm, vaz_hbm, faz_hbm, inc_hbm)):
        copies.append(pltpu.make_async_copy(ref, lines[n], sems.at[NC + n]))
    for n in range(NC):
        part = pl.ds(NC * n, NC)
        copies.append(pltpu.make_async_copy(spin_hbm.at[part], spin.at[part], sems.at[2 * NC + n]))
    copies.append(pltpu.make_async_copy(edge_hbm, edge, sems.at[3 * NC]))
    copies.append(pltpu.make_async_copy(cells_hbm, cells, sems.at[3 * NC + 1]))
    for copy in copies:
        copy.start()
    read = tile_reader(conv, spin, edge, lines)
    lane = lax.broadcasted_iota(jnp.int32, (SUB, LANES), 1)
    row = lax.broadcasted_iota(jnp.int32, (SUB, LANES), 0)
    blank = jnp.zeros((SUB, LANES), jnp.float32)
    first = [[blank] * PACKS for _ in range(2)]
    last = [[blank] * PACKS for _ in range(2)]
    late = list(range(SKEW, VISC)) + [EDGE, FLUID]
    for value in [v for v in range(VALUES) if v not in late] + late:
        for group, begin in enumerate([NC * n for n in range(NC)] + [VISC, FLUX, VAZ, FAZ, INC]):
            if value == begin:
                copies[group].wait()
        if value == late[0]:
            for copy in copies[2 * NC :]:
                copy.wait()
        pack, slot, width = slot_of(value)
        low = slot * width
        here = (lane >= low) & (lane < low + width)
        low = (LANES - width + slot * width) % LANES
        there = (lane >= low) & (lane < low + width)
        for t in range(2):
            if value == FLUID:
                one = jnp.ones((SUB, LANES), jnp.float32)
                for p in range(SOLID_MOST if t == 0 else 0):
                    one = jnp.where(row == p, jnp.where(cells[p] == 0, 1.0, 0.0).astype(jnp.float32), one)
                two = one
            else:
                one, two = read(value, t, 0), read(value, t, 1)
                if slot:
                    one, two = pltpu.roll(one, slot * width, 1), pltpu.roll(two, slot * width, 1)
            first[t][pack] = jnp.where(here, one, first[t][pack])
            last[t][pack] = jnp.where(there, two, last[t][pack])
    for pack in range(PACKS):
        for t in range(2):
            rows = pl.ds(SUB * t, SUB)
            one = mirror(jnp.where(core == 0, first[t][pack], first[1 - t][pack]), core)
            two = mirror(jnp.where(core == 0, last[t][pack], last[1 - t][pack]), core)
            even_out[pack, rows, :] = jnp.where(odd_place, one, two)
            odd_out[pack, rows, :] = jnp.where(odd_place, two, one)


def factor(matrix):
    work = [list(row) for row in matrix]
    scale = []
    for p in range(NC):
        scale.append(1.0 / work[p][p])
        for i in range(p + 1, NC):
            work[i][p] = work[i][p] * scale[p]
            for j in range(p + 1, NC):
                work[i][j] = work[i][j] - work[i][p] * work[p][j]
    for p in range(NC):
        work[p][p] = scale[p]
    return work


def substitute(work, side):
    side = list(side)
    for p in range(NC):
        for i in range(p + 1, NC):
            side[i] = side[i] - work[i][p] * side[p]
    for i in reversed(range(NC)):
        for j in range(i + 1, NC):
            side[i] = side[i] - work[i][j] * side[j]
        side[i] = side[i] * work[i][i]
    return side


def dot(row, column):
    terms = [a * b for a, b in zip(row, column)]
    return (terms[0] + terms[1]) + (terms[2] + terms[3]) + terms[4]


def times(matrix, vector):
    return [dot(row, vector) for row in matrix]


def product(left, right):
    columns = [[right[i][j] for i in range(NC)] for j in range(NC)]
    return [[dot(left[i], columns[j]) for j in range(NC)] for i in range(NC)]


def put(cells, value, t, place, chain, tile):
    is_a = chain == 0
    copies = [(value, 1, 0 if value < SKEW or VISC <= value < VISC + NC else 1)]
    if FLUX <= value < FLUX + NC:
        copies.append((value - FLUX + BELOW, 2, 0))
    for target, slot_a, slot_b in copies:
        if value < SKEW:
            target = jnp.where(is_a, value, value % NC * NC + value // NC)
            tile = tile * jnp.where(is_a, 1.0, -1.0).astype(jnp.float32)
        start = SUB * (SUB * t + jnp.where(is_a, slot_a, slot_b)) + 2 * place + chain
        cells[target, pl.ds(start, SUB, stride=SUB), :] = tile


def put_halo(cells, halo, place, chain):
    for value in range(VALUES):
        if value == FLUID:
            continue
        pack, slot, width = slot_of(value)
        for t in range(2):
            tile = halo[pack, pl.ds(SUB * t, SUB), :]
            if slot:
                tile = pltpu.roll(tile, LANES - slot * width, 1)
            put(cells, value, t, place, chain, tile)


def collect_kernel(bulk, sib_bulk, edge, halo_even, sib_even, cells):
    core = lax.axis_index("wn")
    even_place = 2 + lax.rem(lax.axis_index("az"), 2)
    for chain, array, halo in ((core, bulk, halo_even), (1 - core, sib_bulk, sib_even)):
        conv, spin, lines = parts_of(array)
        read = tile_reader(conv, spin, edge, lines)
        for value in range(VALUES):
            if value == FLUID:
                continue
            for t in range(2):
                for lt in range(2):
                    tile = mirror(read(value, t, lt), chain)
                    put(cells, value, jnp.bitwise_xor(t, chain), lt, chain, tile)
        put_halo(cells, halo, even_place, chain)


def main_kernel(points, *refs):
    cells_in, halo_odd, sib_odd, out_inc, out_defect, cells = refs[0:6]
    couple, conv_face, visc_face, diagonal, skews, lu, sides, solved, vmin, vplus, azd, src, out_cells = refs[6:]

    core = lax.axis_index("wn")
    odd_place = lax.rem(lax.axis_index("az"), 2)
    row = lax.broadcasted_iota(jnp.int32, (SUB, LANES), 0)
    lane = lax.broadcasted_iota(jnp.int32, (SUB, LANES), 1)
    is_a = lax.rem(row, 2) == 0
    put_halo(cells, halo_odd, 3 - odd_place, core)
    put_halo(cells, sib_odd, 3 - odd_place, 1 - core)

    def at(value, k):
        return cells[value, pl.ds(SUB * (k + 1), SUB), :]

    def before(x):
        y = pltpu.roll(x, S, 1)
        return jnp.where(lane < S, pltpu.roll(y, 2, 0), y)

    def after(x):
        y = pltpu.roll(x, LANES - S, 1)
        return jnp.where(lane >= LANES - S, pltpu.roll(y, SUB - 2, 0), y)

    def swap(x):
        return jnp.where(is_a, pltpu.roll(x, SUB - 1, 0), pltpu.roll(x, 1, 0))

    edges = at(EDGE, 0)

    fluid_pack, fluid_slot, fluid_width = slot_of(FLUID)
    fluid_tile = jnp.where(core == 0, halo_odd[fluid_pack, 0:SUB, :], sib_odd[fluid_pack, 0:SUB, :])
    fluid_lane = jnp.where(odd_place == 0, (fluid_slot - 1) * fluid_width, fluid_slot * fluid_width)
    fluid_tile = jnp.max(jnp.where(lane == fluid_lane, fluid_tile, 0.0), axis=1, keepdims=True)

    def fluid(k):
        return jnp.where(is_a, jnp.broadcast_to(fluid_tile[k : k + 1, :], (SUB, LANES)), 1.0)

    def edge_scale(face_a, face_b):
        face = jnp.where(is_a, float(face_a), float(face_b))
        return jnp.where(face < edges, 1.0, OUTER_SCALE)

    one = jnp.ones((SUB, LANES), jnp.float32)
    total = 2 * points
    last = points - 1
    previous = None
    for k in range(points):
        solid = k < SOLID_MOST
        if solid:
            keep = [fluid(k)] * (NC - 1) + [one]
            keep_above = [fluid(k + 1) if k + 1 < SOLID_MOST else one] * (NC - 1) + [one]
        if k < last:
            conv_out = [[at(a * NC + b, k) for b in range(NC)] for a in range(NC)]
            visc_out = [at(VISC + c, k) for c in range(NC)]
        else:
            face = [[at(a * NC + b, k) for b in range(NC)] for a in range(NC)]
            conv_out = [[jnp.where(is_a, face[a][b], -pltpu.roll(face[b][a], 1, 0)) for b in range(NC)] for a in range(NC)]
            raw = [at(VISC + c, k) for c in range(NC)]
            visc_out = [jnp.where(is_a, raw[c], pltpu.roll(raw[c], 1, 0)) for c in range(NC)]
        scale = edge_scale(k, total - 2 - k)
        visc_out = [visc_out[c] * scale for c in range(NC)]
        if solid:
            conv_out = [[conv_out[a][b] * (keep[a] * keep_above[b]) for b in range(NC)] for a in range(NC)]
            visc_out = [visc_out[c] * (keep[c] * keep_above[c]) for c in range(NC)]
        if k == 0:
            scale = edge_scale(0, total - 1)
            visc_in = [jnp.where(is_a, 0.0, at(VISC + c, -1) * scale) for c in range(NC)]

        vm, vp, az_diag, source, side = [], [], [], [], []
        for c in range(NC):
            here = at(VAZ + c, k)
            vm.append(before(here) * keep[c] if solid else before(here))
            vp.append(here * keep[c] if solid else here)
            az_diag.append(vm[c] + vp[c] + (1.0 - keep[c]) if solid else vm[c] + vp[c])
            flux_here, flux_below = at(FLUX + c, k), at(BELOW + c, k)
            if k == 0:
                flux_below = jnp.where(is_a, 0.0, flux_below)
            elif k == last:
                flux_below = jnp.where(is_a, flux_below, pltpu.roll(flux_here, 1, 0))
            flux_side = at(FAZ + c, k)
            flow = flux_below - flux_here + before(flux_side) - flux_side
            source.append(flow * keep[c] if solid else flow)
            start = at(INC + c, k)
            side.append(source[c] + (vm[c] * before(start) + vp[c] * after(start)))
            vmin[k * NC + c], vplus[k * NC + c] = vm[c], vp[c]
            azd[k * NC + c], src[k * NC + c] = az_diag[c], source[c]

        matrix = [[None] * NC for _ in range(NC)]
        for c in range(NC):
            matrix[c][c] = visc_in[c] + visc_out[c] + az_diag[c]
        for n, (a, b) in enumerate(PAIRS):
            skew = at(SKEW + n, k)
            if solid:
                skew = skew * (keep[a] * keep[b])
            skews[k * len(PAIRS) + n] = skew
            matrix[a][b], matrix[b][a] = skew, -skew
        up = [[conv_out[a][b] - visc_out[a] if a == b else conv_out[a][b] for b in range(NC)] for a in range(NC)]
        for a in range(NC):
            diagonal[k * NC + a], visc_face[k * NC + a] = matrix[a][a], visc_out[a]
            for b in range(NC):
                conv_face[k * 25 + a * NC + b] = conv_out[a][b]
        if previous is not None:
            conv_in, couple_in, y_in = previous
            low = [[-visc_in[a] - conv_in[a][a] if a == b else -conv_in[b][a] for b in range(NC)] for a in range(NC)]
            moved = product(low, couple_in)
            matrix = [[matrix[a][b] - moved[a][b] for b in range(NC)] for a in range(NC)]
            shift = times(low, y_in)
            side = [side[c] - shift[c] for c in range(NC)]
        work = factor(matrix)
        columns = [substitute(work, [up[i][j] for i in range(NC)]) for j in range(NC)]
        couple_now = [[columns[j][i] for j in range(NC)] for i in range(NC)]
        y = substitute(work, side)
        for a in range(NC):
            sides[k * NC + a] = y[a]
            for b in range(NC):
                lu[k * 25 + a * NC + b] = work[a][b]
                couple[k * 25 + a * NC + b] = couple_now[a][b]
        previous = (conv_out, couple_now, y)
        visc_in = visc_out

    def block(ref, k):
        return [[ref[k * 25 + a * NC + b] for b in range(NC)] for a in range(NC)]

    def below(k, x):
        face, visc = block(conv_face, k - 1), vector(visc_face, k - 1)
        return [visc[c] * x[c] + dot([face[r][c] for r in range(NC)], x) for c in range(NC)]

    def vector(ref, k):
        return [ref[k * NC + c] for c in range(NC)]

    couple_end = couple_now
    crossed = product(couple_end, [[swap(couple_end[a][b]) for b in range(NC)] for a in range(NC)])
    meeting = factor([[(1.0 if a == b else 0.0) - crossed[a][b] for b in range(NC)] for a in range(NC)])

    def finish(y):
        shift = times(couple_end, [swap(v) for v in y])
        x = substitute(meeting, [y[c] - shift[c] for c in range(NC)])
        for c in range(NC):
            solved[last * NC + c] = x[c]
        for k in reversed(range(last)):
            shift = times(block(couple, k), x)
            y_here = vector(sides, k)
            x = [y_here[c] - shift[c] for c in range(NC)]
            for c in range(NC):
                solved[k * NC + c] = x[c]

    finish(y)
    for sweep in range(1, SWEEPS):
        for k in range(points):
            source, vm, vp, x = vector(src, k), vector(vmin, k), vector(vplus, k), vector(solved, k)
            side = [source[c] + (vm[c] * before(x[c]) + vp[c] * after(x[c])) for c in range(NC)]
            if k:
                shift = below(k, y)
                side = [side[c] + shift[c] for c in range(NC)]
            y = substitute(block(lu, k), side)
            for c in range(NC):
                sides[k * NC + c] = y[c]
        finish(y)

    for k in range(points):
        source, vm, vp, x = vector(src, k), vector(vmin, k), vector(vplus, k), vector(solved, k)
        diag = vector(azd, k)
        beyond = vector(solved, k + 1) if k < last else [swap(v) for v in x]
        visc_out, main = vector(visc_face, k), vector(diagonal, k)
        applied = [main[c] * x[c] - visc_out[c] * beyond[c] for c in range(NC)]
        outer = times(block(conv_face, k), beyond)
        applied = [applied[c] + outer[c] for c in range(NC)]
        for n, (a, b) in enumerate(PAIRS):
            skew = skews[k * len(PAIRS) + n]
            applied[a] = applied[a] + skew * x[b]
            applied[b] = applied[b] - skew * x[a]
        if k:
            under = below(k, vector(solved, k - 1))
            applied = [applied[c] - under[c] for c in range(NC)]
        place = jnp.where(core == 0, k % SUB, SUB - 1 - k % SUB)
        t = jnp.where(core == 0, k // SUB, 1 - k // SUB)
        for c in range(NC):
            offline = vm[c] * before(x[c]) + vp[c] * after(x[c])
            defect = (source[c] + offline - applied[c]) / diag[c]
            out_cells[2 * c + t, pl.ds(place, SUB, stride=SUB), :] = x[c]
            out_cells[2 * (NC + c) + t, pl.ds(place, SUB, stride=SUB), :] = defect
    for c in range(NC):
        for t in range(2):
            for lt in range(2):
                start = pl.multiple_of(SUB * (2 * lt + core), SUB)
                rows, lanes = pl.ds(SUB * t, SUB), pl.ds(LANES * lt, LANES)
                out_inc[c, rows, lanes] = out_cells[2 * c + t, pl.ds(start, SUB), :]
                out_defect[c, rows, lanes] = out_cells[2 * (NC + c) + t, pl.ds(start, SUB), :]


def per_device(visc_wn, conv_wn, spin, visc_az, flux_wn, flux_az, incr_prev, cell_type, edge_index):
    components, points, line_count = visc_wn.shape
    assert components == NC and points == 2 * SUB and line_count == 2 * LANES
    count = lax.axis_size("az")
    assert count % 2 == 0
    even_pairs = [(a, a ^ 1) for a in range(count)]
    odd_pairs = [(a, (a + 1 if a % 2 else a - 1) % count) for a in range(count)]
    vmem, hbm = (pl.BlockSpec(memory_space=m) for m in (pltpu.VMEM, pltpu.HBM))

    blocks = (NC * NC, points, line_count)
    conv, spin = conv_wn.reshape(blocks), spin.reshape(blocks)
    edge = edge_index.reshape(1, line_count)
    lines = (visc_wn, flux_wn, visc_az, flux_az, incr_prev)
    pack = jax.ShapeDtypeStruct((PACKS, points, LANES), jnp.float32)
    block_array = pltpu.VMEM(blocks, jnp.float32)
    bulk = jax.ShapeDtypeStruct((2 * NC * NC + 5 * NC, points, line_count), jnp.float32)
    from_hbm = [pltpu.with_memory_space_constraint(array, pltpu.HBM) for array in (conv, spin, edge, *lines, cell_type)]
    even, odd, bulk, edge = pl.pallas_call(
        pack_kernel,
        out_shape=(pack, pack, bulk, jax.ShapeDtypeStruct((1, line_count), jnp.int32)),
        in_specs=[hbm] * 9,
        out_specs=(vmem,) * 4,
        scratch_shapes=[pltpu.SMEM((points,), jnp.int32), pltpu.SemaphoreType.DMA((3 * NC + 2,))],
        name="pack_halo",
        compiler_params=pltpu.CompilerParams(vmem_limit_bytes=16 << 20),
    )(*from_hbm)
    halo_even = lax.ppermute(even, "az", even_pairs)
    halo_odd = lax.ppermute(odd, "az", odd_pairs)

    def cross(array):
        return lax.ppermute(array, "wn", [(0, 1), (1, 0)])

    sib_bulk = cross(bulk)
    sib_even, sib_odd = cross(halo_even), cross(halo_odd)

    tiles = jax.ShapeDtypeStruct((STORED, SLOTS * SUB, LANES), jnp.float32)
    cells = pl.pallas_call(
        collect_kernel,
        out_shape=tiles,
        in_specs=[vmem] * 5,
        out_specs=vmem,
        name="collect_lines",
        compiler_params=pltpu.CompilerParams(vmem_limit_bytes=16 << 20),
    )(bulk, sib_bulk, edge, halo_even, sib_even)

    def step(count):
        return pltpu.VMEM((points * count, SUB, LANES), jnp.float32)

    out = jax.ShapeDtypeStruct((NC, points, line_count), jnp.float32)
    increment, defect, _ = pl.pallas_call(
        lambda *refs: main_kernel(points, *refs),
        out_shape=(out, out, tiles),
        in_specs=[vmem] * 3,
        out_specs=(vmem, vmem, vmem),
        input_output_aliases={0: 2},
        scratch_shapes=[step(n) for n in (NC * NC, NC * NC, NC, NC, len(PAIRS), NC * NC)]
        + [step(NC)] * 6
        + [pltpu.VMEM((4 * NC, SUB * SUB, LANES), jnp.float32)],
        name="relax_lines",
        compiler_params=pltpu.CompilerParams(vmem_limit_bytes=24 << 20),
    )(cells, halo_odd, sib_odd)
    return increment, defect


def solution(mesh):
    in_specs = (
        P(None, "wn", "az"),
        P(None, None, "wn", "az"),
        P(None, None, "wn", "az"),
        P(None, "wn", "az"),
        P(None, "wn", "az"),
        P(None, "wn", "az"),
        P(None, "wn", "az"),
        P("wn"),
        P("az"),
    )
    out_specs = (P(None, "wn", "az"), P(None, "wn", "az"))
    return jax.shard_map(
        per_device, mesh=mesh, in_specs=in_specs, out_specs=out_specs, check_vma=False
    )
```

```python
import jax
import jax.numpy as jnp
from jax import lax
from jax.experimental import pallas as pl
from jax.experimental.pallas import tpu as pltpu
from jax.sharding import PartitionSpec as P

S = 8
SWEEPS = 2
OUTER_SCALE = 0.25
NC = 5
LANES = 128
SUB = 8
NEAR = 2 * S
FAR = 3 * S

CONV, SKEW, VISC, FLUX, EDGE, FLUID = 0, 25, 35, 40, 45, 46
NEAR_VALUES = 47
VAZ, FAZ, INC = 47, 52, 57
VALUES = 62
BELOW, STORED = 62, 67
SLOTS = 18
SOLID_MOST = 4
NEAR_SLOTS = LANES // NEAR
FAR_SLOTS = LANES // FAR
NEAR_PACKS = -(-NEAR_VALUES // NEAR_SLOTS)
FAR_PACKS = -(-(VALUES - NEAR_VALUES) // FAR_SLOTS)
PACKS = NEAR_PACKS + FAR_PACKS
PAIRS = [(a, b) for a in range(NC) for b in range(a + 1, NC)]


def slot_of(value):
    if value < NEAR_VALUES:
        return value // NEAR_SLOTS, value % NEAR_SLOTS, NEAR
    other = value - NEAR_VALUES
    return NEAR_PACKS + other // FAR_SLOTS, other % FAR_SLOTS, FAR


def tile_reader(conv, spin, edge, lines):
    def read(value, t, lt):
        rows, lanes = pl.ds(SUB * t, SUB), pl.ds(LANES * lt, LANES)
        if value < SKEW:
            return conv[value, rows, lanes]
        if value < VISC:
            a, b = PAIRS[value - SKEW]
            return spin[a * NC + b, rows, lanes] - spin[b * NC + a, rows, lanes]
        if value == EDGE:
            return jnp.broadcast_to(edge[0:1, lanes].astype(jnp.float32), (SUB, LANES))
        for first, ref in zip((VISC, FLUX, VAZ, FAZ, INC), lines):
            if first <= value < first + NC:
                return ref[value - first, rows, lanes]

    return read


def parts_of(ref):
    lines = [ref.at[pl.ds(2 * NC * NC + NC * n, NC)] for n in range(5)]
    return ref.at[pl.ds(0, NC * NC)], ref.at[pl.ds(NC * NC, NC * NC)], lines


def mirror(tile, chain):
    row = lax.broadcasted_iota(jnp.int32, (SUB, LANES), 0)
    return jnp.take_along_axis(tile, jnp.where(chain == 0, row, SUB - 1 - row), axis=0)


def pack_kernel(conv_hbm, spin_hbm, edge_hbm, visc_hbm, flux_hbm, vaz_hbm, faz_hbm, inc_hbm, cells_hbm,
                even_out, odd_out, bulk, edge, cells, sems):
    odd_place = lax.rem(lax.axis_index("az"), 2) == 1
    core = lax.axis_index("wn")
    conv, spin, lines = parts_of(bulk)
    copies = []
    copies.append(pltpu.make_async_copy(conv_hbm, conv, sems.at[0]))
    for n, ref in enumerate((visc_hbm, flux_hbm, vaz_hbm, faz_hbm, inc_hbm)):
        copies.append(pltpu.make_async_copy(ref, lines[n], sems.at[1 + n]))
    copies.append(pltpu.make_async_copy(spin_hbm, spin, sems.at[NC + 1]))
    copies.append(pltpu.make_async_copy(edge_hbm, edge, sems.at[NC + 2]))
    copies.append(pltpu.make_async_copy(cells_hbm, cells, sems.at[NC + 3]))
    for copy in copies:
        copy.start()
    read = tile_reader(conv, spin, edge, lines)
    lane = lax.broadcasted_iota(jnp.int32, (SUB, LANES), 1)
    row = lax.broadcasted_iota(jnp.int32, (SUB, LANES), 0)
    blank = jnp.zeros((SUB, LANES), jnp.float32)
    first = [[blank] * PACKS for _ in range(2)]
    last = [[blank] * PACKS for _ in range(2)]
    late = list(range(SKEW, VISC)) + [EDGE, FLUID]
    for value in [v for v in range(VALUES) if v not in late] + late:
        for group, begin in enumerate([CONV, VISC, FLUX, VAZ, FAZ, INC]):
            if value == begin:
                copies[group].wait()
        if value == late[0]:
            for copy in copies[NC + 1 :]:
                copy.wait()
        pack, slot, width = slot_of(value)
        low = slot * width
        here = (lane >= low) & (lane < low + width)
        low = (LANES - width + slot * width) % LANES
        there = (lane >= low) & (lane < low + width)
        for t in range(2):
            if value == FLUID:
                one = jnp.ones((SUB, LANES), jnp.float32)
                for p in range(SOLID_MOST if t == 0 else 0):
                    one = jnp.where(row == p, jnp.where(cells[p] == 0, 1.0, 0.0).astype(jnp.float32), one)
                two = one
            else:
                one = jnp.where(lane < LANES // 2, read(value, t, 0), read(value, t, 1))
                if slot:
                    one = pltpu.roll(one, slot * width, 1)
                two = one
            first[t][pack] = jnp.where(here, one, first[t][pack])
            last[t][pack] = jnp.where(there, two, last[t][pack])
    for pack in range(PACKS):
        for t in range(2):
            rows = pl.ds(SUB * t, SUB)
            one = mirror(jnp.where(core == 0, first[t][pack], first[1 - t][pack]), core)
            two = mirror(jnp.where(core == 0, last[t][pack], last[1 - t][pack]), core)
            even_out[pack, rows, :] = jnp.where(odd_place, one, two)
            odd_out[pack, rows, :] = jnp.where(odd_place, two, one)


def factor(matrix):
    work = [list(row) for row in matrix]
    scale = []
    for p in range(NC):
        scale.append(1.0 / work[p][p])
        for i in range(p + 1, NC):
            work[i][p] = work[i][p] * scale[p]
            for j in range(p + 1, NC):
                work[i][j] = work[i][j] - work[i][p] * work[p][j]
    for p in range(NC):
        work[p][p] = scale[p]
        for j in range(p + 1, NC):
            work[p][j] = work[p][j] * scale[p]
    return work


def substitute(work, side):
    side = list(side)
    for p in range(NC):
        for i in range(p + 1, NC):
            side[i] = side[i] - work[i][p] * side[p]
    side = [side[p] * work[p][p] for p in range(NC)]
    for p in reversed(range(NC)):
        for i in range(p):
            side[i] = side[i] - work[i][p] * side[p]
    return side


def dot(row, column):
    terms = [a * b for a, b in zip(row, column)]
    return (terms[0] + terms[1]) + (terms[2] + terms[3]) + terms[4]


def times(matrix, vector):
    return [dot(row, vector) for row in matrix]


def product(left, right):
    columns = [[right[i][j] for i in range(NC)] for j in range(NC)]
    return [[dot(left[i], columns[j]) for j in range(NC)] for i in range(NC)]


def put(cells, value, t, place, chain, tile):
    is_a = chain == 0
    copies = [(value, 1, 0 if value < SKEW or VISC <= value < VISC + NC else 1)]
    if FLUX <= value < FLUX + NC:
        copies.append((value - FLUX + BELOW, 2, 0))
    for target, slot_a, slot_b in copies:
        if value < SKEW:
            target = jnp.where(is_a, value, value % NC * NC + value // NC)
            tile = tile * jnp.where(is_a, 1.0, -1.0).astype(jnp.float32)
        start = SUB * (SUB * t + jnp.where(is_a, slot_a, slot_b)) + 2 * place + chain
        cells[target, pl.ds(start, SUB, stride=SUB), :] = tile


def put_halo(cells, halo, place, chain):
    for value in range(VALUES):
        if value == FLUID:
            continue
        pack, slot, width = slot_of(value)
        for t in range(2):
            tile = halo[pack, pl.ds(SUB * t, SUB), :]
            if slot:
                tile = pltpu.roll(tile, LANES - slot * width, 1)
            put(cells, value, t, place, chain, tile)


def collect_kernel(bulk, sib_bulk, edge, halo_even, sib_even, halo_odd, cells):
    core = lax.axis_index("wn")
    even_place = 2 + lax.rem(lax.axis_index("az"), 2)
    for chain, array, halo in ((core, bulk, halo_even), (1 - core, sib_bulk, sib_even)):
        conv, spin, lines = parts_of(array)
        read = tile_reader(conv, spin, edge, lines)
        for value in range(VALUES):
            if value == FLUID:
                continue
            for t in range(2):
                for lt in range(2):
                    tile = mirror(read(value, t, lt), chain)
                    put(cells, value, jnp.bitwise_xor(t, chain), lt, chain, tile)
        put_halo(cells, halo, even_place, chain)
    put_halo(cells, halo_odd, 5 - even_place, core)


def main_kernel(points, *refs):
    cells_in, halo_odd, sib_odd, out_inc, out_defect, cells = refs[0:6]
    couple, conv_face, skews, lu, diagonal, upper_diag, lower_diag, sides, solved, vmin, vplus, azd, src, out_cells = refs[6:]

    core = lax.axis_index("wn")
    odd_place = lax.rem(lax.axis_index("az"), 2)
    row = lax.broadcasted_iota(jnp.int32, (SUB, LANES), 0)
    lane = lax.broadcasted_iota(jnp.int32, (SUB, LANES), 1)
    is_a = lax.rem(row, 2) == 0
    put_halo(cells, sib_odd, 3 - odd_place, 1 - core)

    def at(value, k):
        return cells[value, pl.ds(SUB * (k + 1), SUB), :]

    def before(x):
        y = pltpu.roll(x, S, 1)
        return jnp.where(lane < S, pltpu.roll(y, 2, 0), y)

    def after(x):
        y = pltpu.roll(x, LANES - S, 1)
        return jnp.where(lane >= LANES - S, pltpu.roll(y, SUB - 2, 0), y)

    def swap(x):
        return jnp.where(is_a, pltpu.roll(x, SUB - 1, 0), pltpu.roll(x, 1, 0))

    edges = at(EDGE, 0)

    fluid_pack, fluid_slot, fluid_width = slot_of(FLUID)
    fluid_tile = jnp.where(core == 0, halo_odd[fluid_pack, 0:SUB, :], sib_odd[fluid_pack, 0:SUB, :])
    fluid_lane = jnp.where(odd_place == 0, (fluid_slot - 1) * fluid_width, fluid_slot * fluid_width)
    fluid_tile = jnp.max(jnp.where(lane == fluid_lane, fluid_tile, 0.0), axis=1, keepdims=True)

    def fluid(k):
        return jnp.where(is_a, jnp.broadcast_to(fluid_tile[k : k + 1, :], (SUB, LANES)), 1.0)

    def edge_scale(face_a, face_b):
        face = jnp.where(is_a, float(face_a), float(face_b))
        return jnp.where(face < edges, 1.0, OUTER_SCALE)

    one = jnp.ones((SUB, LANES), jnp.float32)
    total = 2 * points
    last = points - 1
    previous = None
    for k in range(points):
        solid = k < SOLID_MOST
        if solid:
            keep = [fluid(k)] * (NC - 1) + [one]
            keep_above = [fluid(k + 1) if k + 1 < SOLID_MOST else one] * (NC - 1) + [one]
        if k < last:
            conv_out = [[at(a * NC + b, k) for b in range(NC)] for a in range(NC)]
            visc_out = [at(VISC + c, k) for c in range(NC)]
        else:
            face = [[at(a * NC + b, k) for b in range(NC)] for a in range(NC)]
            conv_out = [[jnp.where(is_a, face[a][b], -pltpu.roll(face[b][a], 1, 0)) for b in range(NC)] for a in range(NC)]
            raw = [at(VISC + c, k) for c in range(NC)]
            visc_out = [jnp.where(is_a, raw[c], pltpu.roll(raw[c], 1, 0)) for c in range(NC)]
        scale = edge_scale(k, total - 2 - k)
        visc_out = [visc_out[c] * scale for c in range(NC)]
        if solid:
            conv_out = [[conv_out[a][b] * (keep[a] * keep_above[b]) for b in range(NC)] for a in range(NC)]
            visc_out = [visc_out[c] * (keep[c] * keep_above[c]) for c in range(NC)]
        if k == 0:
            scale = edge_scale(0, total - 1)
            visc_in = [jnp.where(is_a, 0.0, at(VISC + c, -1) * scale) for c in range(NC)]

        vm, vp, az_diag, source, side = [], [], [], [], []
        for c in range(NC):
            here = at(VAZ + c, k)
            vm.append(before(here) * keep[c] if solid else before(here))
            vp.append(here * keep[c] if solid else here)
            az_diag.append(vm[c] + vp[c] + (1.0 - keep[c]) if solid else vm[c] + vp[c])
            flux_here, flux_below = at(FLUX + c, k), at(BELOW + c, k)
            if k == 0:
                flux_below = jnp.where(is_a, 0.0, flux_below)
            elif k == last:
                flux_below = jnp.where(is_a, flux_below, pltpu.roll(flux_here, 1, 0))
            flux_side = at(FAZ + c, k)
            flow = flux_below - flux_here + before(flux_side) - flux_side
            source.append(flow * keep[c] if solid else flow)
            start = at(INC + c, k)
            side.append(source[c] + (vm[c] * before(start) + vp[c] * after(start)))
            vmin[k * NC + c], vplus[k * NC + c] = vm[c], vp[c]
            azd[k * NC + c], src[k * NC + c] = az_diag[c], source[c]

        matrix = [[None] * NC for _ in range(NC)]
        for c in range(NC):
            matrix[c][c] = visc_in[c] + visc_out[c] + az_diag[c]
            diagonal[k * NC + c] = matrix[c][c]
        up = [[conv_out[a][b] - visc_out[a] if a == b else conv_out[a][b] for b in range(NC)] for a in range(NC)]
        low = [[conv_out[a][b] + visc_out[a] if a == b else conv_out[a][b] for b in range(NC)] for a in range(NC)]
        for a in range(NC):
            upper_diag[k * NC + a], lower_diag[k * NC + a] = up[a][a], low[a][a]
            for b in range(NC):
                if a != b:
                    conv_face[k * 25 + a * NC + b] = conv_out[a][b]
        if previous is not None:
            low_in, couple_in, y_in = previous
            moved = product([[low_in[b][a] for b in range(NC)] for a in range(NC)], couple_in)
            shift = times([[low_in[b][a] for b in range(NC)] for a in range(NC)], y_in)
            side = [side[c] + shift[c] for c in range(NC)]
            for c in range(NC):
                matrix[c][c] = matrix[c][c] + moved[c][c]
        for n, (a, b) in enumerate(PAIRS):
            skew = at(SKEW + n, k)
            if solid:
                skew = skew * (keep[a] * keep[b])
            skews[k * len(PAIRS) + n] = skew
            if previous is None:
                matrix[a][b], matrix[b][a] = skew, -skew
            else:
                matrix[a][b], matrix[b][a] = moved[a][b] + skew, moved[b][a] - skew
        work = factor(matrix)
        columns = [substitute(work, [up[i][j] for i in range(NC)]) for j in range(NC)]
        couple_now = [[columns[j][i] for j in range(NC)] for i in range(NC)]
        y = substitute(work, side)
        for a in range(NC):
            sides[k * NC + a] = y[a]
            for b in range(NC):
                lu[k * 25 + a * NC + b] = work[a][b]
                couple[k * 25 + a * NC + b] = couple_now[a][b]
        previous = (low, couple_now, y)
        visc_in = visc_out

    def block(ref, k):
        return [[ref[k * 25 + a * NC + b] for b in range(NC)] for a in range(NC)]

    def vector(ref, k):
        return [ref[k * NC + c] for c in range(NC)]

    def face(diagonal_ref, k):
        corner = vector(diagonal_ref, k)
        return [[corner[a] if a == b else conv_face[k * 25 + a * NC + b] for b in range(NC)] for a in range(NC)]

    def below(k, x, total=(None,) * NC):
        low, total = face(lower_diag, k - 1), list(total)
        for r in reversed(range(NC)):
            for c in range(NC):
                term = low[r][c] * x[r]
                total[c] = term if total[c] is None else total[c] + term
        return total

    couple_end = couple_now
    crossed = product(couple_end, [[swap(couple_end[a][b]) for b in range(NC)] for a in range(NC)])
    meeting = factor([[(1.0 if a == b else 0.0) - crossed[a][b] for b in range(NC)] for a in range(NC)])

    def finish(y, visit):
        shift = times(couple_end, [swap(v) for v in y])
        x = substitute(meeting, [y[c] - shift[c] for c in range(NC)])
        beyond = [swap(v) for v in x]
        for k in reversed(range(points)):
            inner = None
            if k:
                shift = times(block(couple, k - 1), x)
                y_here = vector(sides, k - 1)
                inner = [y_here[c] - shift[c] for c in range(NC)]
            visit(k, inner, x, beyond)
            x, beyond = inner, x

    def offline(k, x):
        vm, vp = vector(vmin, k), vector(vplus, k)
        return [vm[c] * before(x[c]) + vp[c] * after(x[c]) for c in range(NC)]

    def next_side(k, inner, x, beyond):
        source, moved = vector(src, k), offline(k, x)
        for c in range(NC):
            solved[k * NC + c] = source[c] + moved[c]

    def result(k, inner, x, beyond):
        source, moved, diag = vector(src, k), offline(k, x), vector(azd, k)
        main = vector(diagonal, k)
        applied = times(face(upper_diag, k), beyond)
        applied = [applied[c] + main[c] * x[c] for c in range(NC)]
        for n, (a, b) in enumerate(PAIRS):
            skew = skews[k * len(PAIRS) + n]
            applied[a] = applied[a] + skew * x[b]
            applied[b] = applied[b] - skew * x[a]
        if k:
            under = below(k, inner)
            applied = [applied[c] - under[c] for c in range(NC)]
        place = jnp.where(core == 0, k % SUB, SUB - 1 - k % SUB)
        t = jnp.where(core == 0, k // SUB, 1 - k // SUB)
        for c in range(NC):
            defect = (source[c] + moved[c] - applied[c]) / diag[c]
            out_cells[2 * c + t, pl.ds(place, SUB, stride=SUB), :] = x[c]
            out_cells[2 * (NC + c) + t, pl.ds(place, SUB, stride=SUB), :] = defect

    for sweep in range(1, SWEEPS):
        finish(y, next_side)
        for k in range(points):
            side = vector(solved, k)
            if k:
                side = below(k, y, side)
            y = substitute(block(lu, k), side)
            for c in range(NC):
                sides[k * NC + c] = y[c]
    finish(y, result)
    for c in range(NC):
        for t in range(2):
            for lt in range(2):
                start = pl.multiple_of(SUB * (2 * lt + core), SUB)
                rows, lanes = pl.ds(SUB * t, SUB), pl.ds(LANES * lt, LANES)
                out_inc[c, rows, lanes] = out_cells[2 * c + t, pl.ds(start, SUB), :]
                out_defect[c, rows, lanes] = out_cells[2 * (NC + c) + t, pl.ds(start, SUB), :]


def per_device(visc_wn, conv_wn, spin, visc_az, flux_wn, flux_az, incr_prev, cell_type, edge_index):
    components, points, line_count = visc_wn.shape
    assert components == NC and points == 2 * SUB and line_count == 2 * LANES
    count = lax.axis_size("az")
    assert count % 2 == 0
    even_pairs = [(a, a ^ 1) for a in range(count)]
    odd_pairs = [(a, (a + 1 if a % 2 else a - 1) % count) for a in range(count)]
    vmem, hbm = (pl.BlockSpec(memory_space=m) for m in (pltpu.VMEM, pltpu.HBM))

    blocks = (NC * NC, points, line_count)
    conv, spin = conv_wn.reshape(blocks), spin.reshape(blocks)
    edge = edge_index.reshape(1, line_count)
    lines = (visc_wn, flux_wn, visc_az, flux_az, incr_prev)
    pack = jax.ShapeDtypeStruct((PACKS, points, LANES), jnp.float32)
    block_array = pltpu.VMEM(blocks, jnp.float32)
    bulk = jax.ShapeDtypeStruct((2 * NC * NC + 5 * NC, points, line_count), jnp.float32)
    from_hbm = [pltpu.with_memory_space_constraint(array, pltpu.HBM) for array in (conv, spin, edge, *lines, cell_type)]
    even, odd, bulk, edge = pl.pallas_call(
        pack_kernel,
        out_shape=(pack, pack, bulk, jax.ShapeDtypeStruct((1, line_count), jnp.int32)),
        in_specs=[hbm] * 9,
        out_specs=(vmem,) * 4,
        scratch_shapes=[pltpu.SMEM((points,), jnp.int32), pltpu.SemaphoreType.DMA((NC + 4,))],
        name="pack_halo",
        compiler_params=pltpu.CompilerParams(vmem_limit_bytes=16 << 20),
    )(*from_hbm)
    halo_even = lax.ppermute(even, "az", even_pairs)
    halo_odd = lax.ppermute(odd, "az", odd_pairs)

    def cross(array):
        return lax.ppermute(array, "wn", [(0, 1), (1, 0)])

    sib_bulk = cross(bulk)
    sib_even, sib_odd = cross(halo_even), cross(halo_odd)

    tiles = jax.ShapeDtypeStruct((STORED, SLOTS * SUB, LANES), jnp.float32)
    cells = pl.pallas_call(
        collect_kernel,
        out_shape=tiles,
        in_specs=[vmem] * 6,
        out_specs=vmem,
        name="collect_lines",
        compiler_params=pltpu.CompilerParams(vmem_limit_bytes=16 << 20),
    )(bulk, sib_bulk, edge, halo_even, sib_even, halo_odd)

    def step(count):
        return pltpu.VMEM((points * count, SUB, LANES), jnp.float32)

    out = jax.ShapeDtypeStruct((NC, points, line_count), jnp.float32)
    increment, defect, _ = pl.pallas_call(
        lambda *refs: main_kernel(points, *refs),
        out_shape=(out, out, tiles),
        in_specs=[vmem] * 3,
        out_specs=(vmem, vmem, vmem),
        input_output_aliases={0: 2},
        scratch_shapes=[step(n) for n in (NC * NC, NC * NC, len(PAIRS), NC * NC)]
        + [step(NC)] * 9
        + [pltpu.VMEM((4 * NC, SUB * SUB, LANES), jnp.float32)],
        name="relax_lines",
        compiler_params=pltpu.CompilerParams(vmem_limit_bytes=24 << 20),
    )(cells, halo_odd, sib_odd)
    return increment, defect


def solution(mesh):
    in_specs = (
        P(None, "wn", "az"),
        P(None, None, "wn", "az"),
        P(None, None, "wn", "az"),
        P(None, "wn", "az"),
        P(None, "wn", "az"),
        P(None, "wn", "az"),
        P(None, "wn", "az"),
        P("wn"),
        P("az"),
    )
    out_specs = (P(None, "wn", "az"), P(None, "wn", "az"))
    return jax.shard_map(
        per_device, mesh=mesh, in_specs=in_specs, out_specs=out_specs, check_vma=False
    )
```

```python
import jax
import jax.numpy as jnp
from jax import lax
from jax.experimental import pallas as pl
from jax.experimental.pallas import tpu as pltpu
from jax.sharding import PartitionSpec as P

S = 8
SWEEPS = 2
OUTER_SCALE = 0.25
NC = 5
LANES = 128
SUB = 8
NEAR = 2 * S
FAR = 3 * S

CONV, SKEW, VISC, FLUX, EDGE, FLUID = 0, 25, 35, 40, 45, 46
NEAR_VALUES = 47
VAZ, FAZ, INC = 47, 52, 57
VALUES = 62
BELOW, STORED = 62, 67
SLOTS = 19
SOLID_MOST = 4
NEAR_SLOTS = LANES // NEAR
FAR_SLOTS = LANES // FAR
NEAR_PACKS = -(-NEAR_VALUES // NEAR_SLOTS)
FAR_PACKS = -(-(VALUES - NEAR_VALUES) // FAR_SLOTS)
PACKS = NEAR_PACKS + FAR_PACKS
PAIRS = [(a, b) for a in range(NC) for b in range(a + 1, NC)]


def slot_of(value):
    if value < NEAR_VALUES:
        return value // NEAR_SLOTS, value % NEAR_SLOTS, NEAR
    other = value - NEAR_VALUES
    return NEAR_PACKS + other // FAR_SLOTS, other % FAR_SLOTS, FAR


def tile_reader(conv, spin, edge, lines):
    def read(value, t, lt):
        rows, lanes = pl.ds(SUB * t, SUB), pl.ds(LANES * lt, LANES)
        if value < SKEW:
            return conv[value, rows, lanes]
        if value < VISC:
            a, b = PAIRS[value - SKEW]
            return spin[a * NC + b, rows, lanes] - spin[b * NC + a, rows, lanes]
        if value == EDGE:
            return jnp.broadcast_to(edge[0:1, lanes].astype(jnp.float32), (SUB, LANES))
        for first, ref in zip((VISC, FLUX, VAZ, FAZ, INC), lines):
            if first <= value < first + NC:
                return ref[value - first, rows, lanes]

    return read


def parts_of(ref):
    lines = [ref.at[pl.ds(2 * NC * NC + NC * n, NC)] for n in range(5)]
    return ref.at[pl.ds(0, NC * NC)], ref.at[pl.ds(NC * NC, NC * NC)], lines


def mirror(tile, chain):
    row = lax.broadcasted_iota(jnp.int32, (SUB, LANES), 0)
    return jnp.take_along_axis(tile, jnp.where(chain == 0, row, SUB - 1 - row), axis=0)


def pack_kernel(conv_hbm, spin_hbm, edge_hbm, visc_hbm, flux_hbm, vaz_hbm, faz_hbm, inc_hbm, cells_hbm,
                even_out, odd_out, bulk, edge, cells, sems):
    odd_place = lax.rem(lax.axis_index("az"), 2) == 1
    core = lax.axis_index("wn")
    conv, spin, lines = parts_of(bulk)
    copies = []
    copies.append(pltpu.make_async_copy(conv_hbm, conv, sems.at[0]))
    for n, ref in enumerate((visc_hbm, flux_hbm, vaz_hbm, faz_hbm, inc_hbm)):
        copies.append(pltpu.make_async_copy(ref, lines[n], sems.at[1 + n]))
    copies.append(pltpu.make_async_copy(spin_hbm, spin, sems.at[NC + 1]))
    copies.append(pltpu.make_async_copy(edge_hbm, edge, sems.at[NC + 2]))
    copies.append(pltpu.make_async_copy(cells_hbm, cells, sems.at[NC + 3]))
    for copy in copies:
        copy.start()
    read = tile_reader(conv, spin, edge, lines)
    lane = lax.broadcasted_iota(jnp.int32, (SUB, LANES), 1)
    row = lax.broadcasted_iota(jnp.int32, (SUB, LANES), 0)
    blank = jnp.zeros((SUB, LANES), jnp.float32)
    first = [[blank] * PACKS for _ in range(2)]
    last = [[blank] * PACKS for _ in range(2)]
    late = list(range(SKEW, VISC)) + [EDGE, FLUID]
    for value in [v for v in range(VALUES) if v not in late] + late:
        for group, begin in enumerate([CONV, VISC, FLUX, VAZ, FAZ, INC]):
            if value == begin:
                copies[group].wait()
        if value == late[0]:
            for copy in copies[NC + 1 :]:
                copy.wait()
        pack, slot, width = slot_of(value)
        low = slot * width
        here = (lane >= low) & (lane < low + width)
        low = (LANES - width + slot * width) % LANES
        there = (lane >= low) & (lane < low + width)
        for t in range(2):
            if value == FLUID:
                one = jnp.ones((SUB, LANES), jnp.float32)
                for p in range(SOLID_MOST if t == 0 else 0):
                    one = jnp.where(row == p, jnp.where(cells[p] == 0, 1.0, 0.0).astype(jnp.float32), one)
                two = one
            else:
                one = jnp.where(lane < LANES // 2, read(value, t, 0), read(value, t, 1))
                if slot:
                    one = pltpu.roll(one, slot * width, 1)
                two = one
            first[t][pack] = jnp.where(here, one, first[t][pack])
            last[t][pack] = jnp.where(there, two, last[t][pack])
    for pack in range(PACKS):
        for t in range(2):
            rows = pl.ds(SUB * t, SUB)
            one = mirror(jnp.where(core == 0, first[t][pack], first[1 - t][pack]), core)
            two = mirror(jnp.where(core == 0, last[t][pack], last[1 - t][pack]), core)
            even_out[pack, rows, :] = jnp.where(odd_place, one, two)
            odd_out[pack, rows, :] = jnp.where(odd_place, two, one)


def factor(matrix):
    work = [list(row) for row in matrix]
    scale = []
    for p in range(NC):
        scale.append(1.0 / work[p][p])
        for i in range(p + 1, NC):
            work[i][p] = work[i][p] * scale[p]
            for j in range(p + 1, NC):
                work[i][j] = work[i][j] - work[i][p] * work[p][j]
    for p in range(NC):
        work[p][p] = scale[p]
        for j in range(p + 1, NC):
            work[p][j] = work[p][j] * scale[p]
    return work


def substitute(work, side):
    side = list(side)
    for p in range(NC):
        for i in range(p + 1, NC):
            side[i] = side[i] - work[i][p] * side[p]
    side = [side[p] * work[p][p] for p in range(NC)]
    for p in reversed(range(NC)):
        for i in range(p):
            side[i] = side[i] - work[i][p] * side[p]
    return side


def dot(row, column):
    terms = [a * b for a, b in zip(row, column)]
    return (terms[0] + terms[1]) + (terms[2] + terms[3]) + terms[4]


def times(matrix, vector):
    return [dot(row, vector) for row in matrix]


def product(left, right):
    columns = [[right[i][j] for i in range(NC)] for j in range(NC)]
    return [[dot(left[i], columns[j]) for j in range(NC)] for i in range(NC)]


def put(cells, value, t, place, chain, tile):
    is_a = chain == 0
    copies = [(value, 1, 0 if value < SKEW or VISC <= value < VISC + NC else 1)]
    if FLUX <= value < FLUX + NC:
        copies.append((value - FLUX + BELOW, 2, 0))
    for target, slot_a, slot_b in copies:
        if value < SKEW:
            target = jnp.where(is_a, value, value % NC * NC + value // NC)
            tile = tile * jnp.where(is_a, 1.0, -1.0).astype(jnp.float32)
        start = SUB * (SUB * t + jnp.where(is_a, slot_a, slot_b)) + 2 * place + chain
        cells[target, pl.ds(start, SUB, stride=SUB), :] = tile


def put_halo(cells, halo, place, chain):
    for value in range(VALUES):
        if value == FLUID:
            continue
        pack, slot, width = slot_of(value)
        for t in range(2):
            tile = halo[pack, pl.ds(SUB * t, SUB), :]
            if slot:
                tile = pltpu.roll(tile, LANES - slot * width, 1)
            put(cells, value, t, place, chain, tile)


def collect_kernel(bulk, sib_bulk, edge, halo_even, sib_even, halo_odd, cells):
    core = lax.axis_index("wn")
    even_place = 2 + lax.rem(lax.axis_index("az"), 2)
    for chain, array, halo in ((core, bulk, halo_even), (1 - core, sib_bulk, sib_even)):
        conv, spin, lines = parts_of(array)
        read = tile_reader(conv, spin, edge, lines)
        for value in range(VALUES):
            if value == FLUID:
                continue
            for t in range(2):
                for lt in range(2):
                    tile = mirror(read(value, t, lt), chain)
                    put(cells, value, jnp.bitwise_xor(t, chain), lt, chain, tile)
        put_halo(cells, halo, even_place, chain)
    put_halo(cells, halo_odd, 5 - even_place, core)


def main_kernel(points, *refs):
    cells_in, halo_odd, sib_odd, out_inc, out_defect, cells = refs[0:6]
    couple, conv_face, skews, lu, diagonal, upper_diag, lower_diag, sides, solved, vmin, vplus, azd, src, out_cells = refs[6:]

    core = lax.axis_index("wn")
    odd_place = lax.rem(lax.axis_index("az"), 2)
    row = lax.broadcasted_iota(jnp.int32, (SUB, LANES), 0)
    lane = lax.broadcasted_iota(jnp.int32, (SUB, LANES), 1)
    is_a = lax.rem(row, 2) == 0
    put_halo(cells, sib_odd, 3 - odd_place, 1 - core)

    def at(value, k):
        return cells[value, pl.ds(SUB * (k + 1), SUB), :]

    def before(x):
        y = pltpu.roll(x, S, 1)
        return jnp.where(lane < S, pltpu.roll(y, 2, 0), y)

    def after(x):
        y = pltpu.roll(x, LANES - S, 1)
        return jnp.where(lane >= LANES - S, pltpu.roll(y, SUB - 2, 0), y)

    def swap(x):
        return jnp.where(is_a, pltpu.roll(x, SUB - 1, 0), pltpu.roll(x, 1, 0))

    edges = at(EDGE, 0)

    fluid_pack, fluid_slot, fluid_width = slot_of(FLUID)
    fluid_tile = jnp.where(core == 0, halo_odd[fluid_pack, 0:SUB, :], sib_odd[fluid_pack, 0:SUB, :])
    fluid_lane = jnp.where(odd_place == 0, (fluid_slot - 1) * fluid_width, fluid_slot * fluid_width)
    fluid_tile = jnp.max(jnp.where(lane == fluid_lane, fluid_tile, 0.0), axis=1, keepdims=True)

    def fluid(k):
        return jnp.where(is_a, jnp.broadcast_to(fluid_tile[k : k + 1, :], (SUB, LANES)), 1.0)

    def edge_scale(face_a, face_b):
        face = jnp.where(is_a, float(face_a), float(face_b))
        return jnp.where(face < edges, 1.0, OUTER_SCALE)

    one = jnp.ones((SUB, LANES), jnp.float32)
    total = 2 * points
    last = points - 1
    previous = None
    for k in range(points):
        solid = k < SOLID_MOST
        if solid:
            keep = [fluid(k)] * (NC - 1) + [one]
            keep_above = [fluid(k + 1) if k + 1 < SOLID_MOST else one] * (NC - 1) + [one]
        if k < last:
            conv_out = [[at(a * NC + b, k) for b in range(NC)] for a in range(NC)]
            visc_out = [at(VISC + c, k) for c in range(NC)]
        else:
            face = [[at(a * NC + b, k) for b in range(NC)] for a in range(NC)]
            conv_out = [[jnp.where(is_a, face[a][b], -pltpu.roll(face[b][a], 1, 0)) for b in range(NC)] for a in range(NC)]
            raw = [at(VISC + c, k) for c in range(NC)]
            visc_out = [jnp.where(is_a, raw[c], pltpu.roll(raw[c], 1, 0)) for c in range(NC)]
        scale = edge_scale(k, total - 2 - k)
        visc_out = [visc_out[c] * scale for c in range(NC)]
        if solid:
            conv_out = [[conv_out[a][b] * (keep[a] * keep_above[b]) for b in range(NC)] for a in range(NC)]
            visc_out = [visc_out[c] * (keep[c] * keep_above[c]) for c in range(NC)]
        if k == 0:
            scale = edge_scale(0, total - 1)
            visc_in = [jnp.where(is_a, 0.0, at(VISC + c, -1) * scale) for c in range(NC)]

        vm, vp, az_diag, source, side = [], [], [], [], []
        for c in range(NC):
            here = at(VAZ + c, k)
            vm.append(before(here) * keep[c] if solid else before(here))
            vp.append(here * keep[c] if solid else here)
            az_diag.append(vm[c] + vp[c] + (1.0 - keep[c]) if solid else vm[c] + vp[c])
            flux_here, flux_below = at(FLUX + c, k), at(BELOW + c, k)
            if k == 0:
                flux_below = jnp.where(is_a, 0.0, flux_below)
            elif k == last:
                flux_below = jnp.where(is_a, flux_below, pltpu.roll(flux_here, 1, 0))
            flux_side = at(FAZ + c, k)
            flow = flux_below - flux_here + before(flux_side) - flux_side
            source.append(flow * keep[c] if solid else flow)
            start = at(INC + c, k)
            side.append(source[c] + (vm[c] * before(start) + vp[c] * after(start)))
            vmin[k * NC + c], vplus[k * NC + c] = vm[c], vp[c]
            azd[k * NC + c], src[k * NC + c] = az_diag[c], source[c]

        matrix = [[None] * NC for _ in range(NC)]
        for c in range(NC):
            matrix[c][c] = visc_in[c] + visc_out[c] + az_diag[c]
            diagonal[k * NC + c] = matrix[c][c]
        up = [[conv_out[a][b] - visc_out[a] if a == b else conv_out[a][b] for b in range(NC)] for a in range(NC)]
        low = [[conv_out[a][b] + visc_out[a] if a == b else conv_out[a][b] for b in range(NC)] for a in range(NC)]
        for a in range(NC):
            upper_diag[k * NC + a], lower_diag[k * NC + a] = up[a][a], low[a][a]
            for b in range(NC):
                if a != b:
                    conv_face[k * 25 + a * NC + b] = conv_out[a][b]
        if previous is not None:
            low_in, couple_in, y_in = previous
            moved = product([[low_in[b][a] for b in range(NC)] for a in range(NC)], couple_in)
            shift = times([[low_in[b][a] for b in range(NC)] for a in range(NC)], y_in)
            side = [side[c] + shift[c] for c in range(NC)]
            for c in range(NC):
                matrix[c][c] = matrix[c][c] + moved[c][c]
        for n, (a, b) in enumerate(PAIRS):
            skew = at(SKEW + n, k)
            if solid:
                skew = skew * (keep[a] * keep[b])
            skews[k * len(PAIRS) + n] = skew
            if previous is None:
                matrix[a][b], matrix[b][a] = skew, -skew
            else:
                matrix[a][b], matrix[b][a] = moved[a][b] + skew, moved[b][a] - skew
        work = factor(matrix)
        columns = [substitute(work, [up[i][j] for i in range(NC)]) for j in range(NC)]
        couple_now = [[columns[j][i] for j in range(NC)] for i in range(NC)]
        y = substitute(work, side)
        for a in range(NC):
            sides[k * NC + a] = y[a]
            for b in range(NC):
                lu[k * 25 + a * NC + b] = work[a][b]
                couple[k * 25 + a * NC + b] = couple_now[a][b]
        previous = (low, couple_now, y)
        visc_in = visc_out

    def block(ref, k):
        return [[ref[k * 25 + a * NC + b] for b in range(NC)] for a in range(NC)]

    def vector(ref, k):
        return [ref[k * NC + c] for c in range(NC)]

    def face(diagonal_ref, k):
        corner = vector(diagonal_ref, k)
        return [[corner[a] if a == b else conv_face[k * 25 + a * NC + b] for b in range(NC)] for a in range(NC)]

    def below(k, x, total=(None,) * NC):
        low, total = face(lower_diag, k - 1), list(total)
        for r in reversed(range(NC)):
            for c in range(NC):
                term = low[r][c] * x[r]
                total[c] = term if total[c] is None else total[c] + term
        return total

    couple_end = couple_now
    crossed = product(couple_end, [[swap(couple_end[a][b]) for b in range(NC)] for a in range(NC)])
    meeting = factor([[(1.0 if a == b else 0.0) - crossed[a][b] for b in range(NC)] for a in range(NC)])

    def finish(y, visit):
        shift = times(couple_end, [swap(v) for v in y])
        x = substitute(meeting, [y[c] - shift[c] for c in range(NC)])
        beyond = [swap(v) for v in x]
        for k in reversed(range(points)):
            inner = None
            if k:
                shift = times(block(couple, k - 1), x)
                y_here = vector(sides, k - 1)
                inner = [y_here[c] - shift[c] for c in range(NC)]
            visit(k, inner, x, beyond)
            x, beyond = inner, x

    def offline(k, x):
        vm, vp = vector(vmin, k), vector(vplus, k)
        return [vm[c] * before(x[c]) + vp[c] * after(x[c]) for c in range(NC)]

    def next_side(k, inner, x, beyond):
        source, moved = vector(src, k), offline(k, x)
        for c in range(NC):
            solved[k * NC + c] = source[c] + moved[c]

    def result(k, inner, x, beyond):
        source, moved, diag = vector(src, k), offline(k, x), vector(azd, k)
        main = vector(diagonal, k)
        applied = times(face(upper_diag, k), beyond)
        applied = [applied[c] + main[c] * x[c] for c in range(NC)]
        for n, (a, b) in enumerate(PAIRS):
            skew = skews[k * len(PAIRS) + n]
            applied[a] = applied[a] + skew * x[b]
            applied[b] = applied[b] - skew * x[a]
        if k:
            under = below(k, inner)
            applied = [applied[c] - under[c] for c in range(NC)]
        place = jnp.where(core == 0, k % SUB, SUB - 1 - k % SUB)
        t = jnp.where(core == 0, k // SUB, 1 - k // SUB)
        for c in range(NC):
            defect = (source[c] + moved[c] - applied[c]) / diag[c]
            out_cells[2 * c + t, pl.ds(place, SUB, stride=SUB), :] = x[c]
            out_cells[2 * (NC + c) + t, pl.ds(place, SUB, stride=SUB), :] = defect

    for sweep in range(1, SWEEPS):
        finish(y, next_side)
        for k in range(points):
            side = vector(solved, k)
            if k:
                side = below(k, y, side)
            y = substitute(block(lu, k), side)
            for c in range(NC):
                sides[k * NC + c] = y[c]
    finish(y, result)
    for c in range(NC):
        for t in range(2):
            for lt in range(2):
                start = pl.multiple_of(SUB * (2 * lt + core), SUB)
                rows, lanes = pl.ds(SUB * t, SUB), pl.ds(LANES * lt, LANES)
                out_inc[c, rows, lanes] = out_cells[2 * c + t, pl.ds(start, SUB), :]
                out_defect[c, rows, lanes] = out_cells[2 * (NC + c) + t, pl.ds(start, SUB), :]


def per_device(visc_wn, conv_wn, spin, visc_az, flux_wn, flux_az, incr_prev, cell_type, edge_index):
    components, points, line_count = visc_wn.shape
    assert components == NC and points == 2 * SUB and line_count == 2 * LANES
    count = lax.axis_size("az")
    assert count % 2 == 0
    even_pairs = [(a, a ^ 1) for a in range(count)]
    odd_pairs = [(a, (a + 1 if a % 2 else a - 1) % count) for a in range(count)]
    vmem, hbm = (pl.BlockSpec(memory_space=m) for m in (pltpu.VMEM, pltpu.HBM))

    blocks = (NC * NC, points, line_count)
    conv, spin = conv_wn.reshape(blocks), spin.reshape(blocks)
    edge = edge_index.reshape(1, line_count)
    lines = (visc_wn, flux_wn, visc_az, flux_az, incr_prev)
    pack = jax.ShapeDtypeStruct((PACKS, points, LANES), jnp.float32)
    block_array = pltpu.VMEM(blocks, jnp.float32)
    bulk = jax.ShapeDtypeStruct((2 * NC * NC + 5 * NC, points, line_count), jnp.float32)
    from_hbm = [pltpu.with_memory_space_constraint(array, pltpu.HBM) for array in (conv, spin, edge, *lines, cell_type)]
    even, odd, bulk, edge = pl.pallas_call(
        pack_kernel,
        out_shape=(pack, pack, bulk, jax.ShapeDtypeStruct((1, line_count), jnp.int32)),
        in_specs=[hbm] * 9,
        out_specs=(vmem,) * 4,
        scratch_shapes=[pltpu.SMEM((points,), jnp.int32), pltpu.SemaphoreType.DMA((NC + 4,))],
        name="pack_halo",
        compiler_params=pltpu.CompilerParams(vmem_limit_bytes=16 << 20),
    )(*from_hbm)
    halo_even = lax.ppermute(even, "az", even_pairs)
    halo_odd = lax.ppermute(odd, "az", odd_pairs)

    def cross(array):
        return lax.ppermute(array, "wn", [(0, 1), (1, 0)])

    sib_bulk = cross(bulk)
    sib_even, sib_odd = cross(halo_even), cross(halo_odd)

    tiles = jax.ShapeDtypeStruct((STORED, SLOTS * SUB, LANES), jnp.float32)
    cells = pl.pallas_call(
        collect_kernel,
        out_shape=tiles,
        in_specs=[vmem] * 6,
        out_specs=vmem,
        name="collect_lines",
        compiler_params=pltpu.CompilerParams(vmem_limit_bytes=16 << 20),
    )(bulk, sib_bulk, edge, halo_even, sib_even, halo_odd)

    def step(count):
        return pltpu.VMEM((points * count, SUB, LANES), jnp.float32)

    out = jax.ShapeDtypeStruct((NC, points, line_count), jnp.float32)
    increment, defect, _ = pl.pallas_call(
        lambda *refs: main_kernel(points, *refs),
        out_shape=(out, out, tiles),
        in_specs=[vmem] * 3,
        out_specs=(vmem, vmem, vmem),
        input_output_aliases={0: 2},
        scratch_shapes=[step(n) for n in (NC * NC, NC * NC, len(PAIRS), NC * NC)]
        + [step(NC)] * 9
        + [pltpu.VMEM((4 * NC, SUB * SUB + SUB, LANES), jnp.float32)],
        name="relax_lines",
        compiler_params=pltpu.CompilerParams(vmem_limit_bytes=24 << 20),
    )(cells, halo_odd, sib_odd)
    return increment, defect


def solution(mesh):
    in_specs = (
        P(None, "wn", "az"),
        P(None, None, "wn", "az"),
        P(None, None, "wn", "az"),
        P(None, "wn", "az"),
        P(None, "wn", "az"),
        P(None, "wn", "az"),
        P(None, "wn", "az"),
        P("wn"),
        P("az"),
    )
    out_specs = (P(None, "wn", "az"), P(None, "wn", "az"))
    return jax.shard_map(
        per_device, mesh=mesh, in_specs=in_specs, out_specs=out_specs, check_vma=False
    )
```

```python
import jax
import jax.numpy as jnp
from jax import lax
from jax.experimental import pallas as pl
from jax.experimental.pallas import tpu as pltpu
from jax.sharding import PartitionSpec as P

S = 8
SWEEPS = 2
OUTER_SCALE = 0.25
NC = 5
LANES = 128
SUB = 8
NEAR = 2 * S
FAR = 3 * S

CONV, SKEW, VISC, FLUX, EDGE, FLUID = 0, 25, 35, 40, 45, 46
NEAR_VALUES = 47
VAZ, FAZ, INC = 47, 52, 57
VALUES = 62
BELOW, STORED = 62, 67
SLOTS = 19
SOLID_MOST = 4
NEAR_SLOTS = LANES // NEAR
FAR_SLOTS = LANES // FAR
NEAR_PACKS = -(-NEAR_VALUES // NEAR_SLOTS)
FAR_PACKS = -(-(VALUES - NEAR_VALUES) // FAR_SLOTS)
PACKS = NEAR_PACKS + FAR_PACKS
PAIRS = [(a, b) for a in range(NC) for b in range(a + 1, NC)]


def slot_of(value):
    if value < NEAR_VALUES:
        return value // NEAR_SLOTS, value % NEAR_SLOTS, NEAR
    other = value - NEAR_VALUES
    return NEAR_PACKS + other // FAR_SLOTS, other % FAR_SLOTS, FAR


def tile_reader(conv, spin, edge, lines):
    def read(value, t, lt):
        rows, lanes = pl.ds(SUB * t, SUB), pl.ds(LANES * lt, LANES)
        if value < SKEW:
            return conv[value, rows, lanes]
        if value < VISC:
            a, b = PAIRS[value - SKEW]
            return spin[a * NC + b, rows, lanes] - spin[b * NC + a, rows, lanes]
        if value == EDGE:
            return jnp.broadcast_to(edge[0:1, lanes].astype(jnp.float32), (SUB, LANES))
        for first, ref in zip((VISC, FLUX, VAZ, FAZ, INC), lines):
            if first <= value < first + NC:
                return ref[value - first, rows, lanes]

    return read


def parts_of(ref):
    lines = [ref.at[pl.ds(2 * NC * NC + NC * n, NC)] for n in range(5)]
    return ref.at[pl.ds(0, NC * NC)], ref.at[pl.ds(NC * NC, NC * NC)], lines


def mirror(tile, chain):
    row = lax.broadcasted_iota(jnp.int32, (SUB, LANES), 0)
    return jnp.take_along_axis(tile, jnp.where(chain == 0, row, SUB - 1 - row), axis=0)


def pack_kernel(conv_hbm, spin_hbm, edge_hbm, visc_hbm, flux_hbm, vaz_hbm, faz_hbm, inc_hbm, cells_hbm,
                even_out, odd_out, bulk, edge, cells, sems):
    odd_place = lax.rem(lax.axis_index("az"), 2) == 1
    core = lax.axis_index("wn")
    conv, spin, lines = parts_of(bulk)
    copies = []
    copies.append(pltpu.make_async_copy(conv_hbm, conv, sems.at[0]))
    for n, ref in enumerate((visc_hbm, flux_hbm, vaz_hbm, faz_hbm, inc_hbm)):
        copies.append(pltpu.make_async_copy(ref, lines[n], sems.at[1 + n]))
    copies.append(pltpu.make_async_copy(spin_hbm, spin, sems.at[NC + 1]))
    copies.append(pltpu.make_async_copy(edge_hbm, edge, sems.at[NC + 2]))
    copies.append(pltpu.make_async_copy(cells_hbm, cells, sems.at[NC + 3]))
    for copy in copies:
        copy.start()
    read = tile_reader(conv, spin, edge, lines)
    lane = lax.broadcasted_iota(jnp.int32, (SUB, LANES), 1)
    row = lax.broadcasted_iota(jnp.int32, (SUB, LANES), 0)
    blank = jnp.zeros((SUB, LANES), jnp.float32)
    first = [[blank] * PACKS for _ in range(2)]
    last = [[blank] * PACKS for _ in range(2)]
    late = list(range(SKEW, VISC)) + [EDGE, FLUID]
    for value in [v for v in range(VALUES) if v not in late] + late:
        for group, begin in enumerate([CONV, VISC, FLUX, VAZ, FAZ, INC]):
            if value == begin:
                copies[group].wait()
        if value == late[0]:
            for copy in copies[NC + 1 :]:
                copy.wait()
        pack, slot, width = slot_of(value)
        low = slot * width
        here = (lane >= low) & (lane < low + width)
        low = (LANES - width + slot * width) % LANES
        there = (lane >= low) & (lane < low + width)
        for t in range(2):
            if value == FLUID:
                one = jnp.ones((SUB, LANES), jnp.float32)
                for p in range(SOLID_MOST if t == 0 else 0):
                    one = jnp.where(row == p, jnp.where(cells[p] == 0, 1.0, 0.0).astype(jnp.float32), one)
                two = one
            else:
                one = jnp.where(lane < LANES // 2, read(value, t, 0), read(value, t, 1))
                if slot:
                    one = pltpu.roll(one, slot * width, 1)
                two = one
            first[t][pack] = jnp.where(here, one, first[t][pack])
            last[t][pack] = jnp.where(there, two, last[t][pack])
    for pack in range(PACKS):
        for t in range(2):
            rows = pl.ds(SUB * t, SUB)
            one = mirror(jnp.where(core == 0, first[t][pack], first[1 - t][pack]), core)
            two = mirror(jnp.where(core == 0, last[t][pack], last[1 - t][pack]), core)
            even_out[pack, rows, :] = jnp.where(odd_place, one, two)
            odd_out[pack, rows, :] = jnp.where(odd_place, two, one)


def factor(matrix):
    work = [list(row) for row in matrix]
    scale = []
    for p in range(NC):
        scale.append(1.0 / work[p][p])
        for i in range(p + 1, NC):
            work[i][p] = work[i][p] * scale[p]
            for j in range(p + 1, NC):
                work[i][j] = work[i][j] - work[i][p] * work[p][j]
    for p in range(NC):
        work[p][p] = scale[p]
        for j in range(p + 1, NC):
            work[p][j] = work[p][j] * scale[p]
    return work


def substitute(work, side):
    side = list(side)
    for p in range(NC):
        for i in range(p + 1, NC):
            side[i] = side[i] - work[i][p] * side[p]
    side = [side[p] * work[p][p] for p in range(NC)]
    for p in reversed(range(NC)):
        for i in range(p):
            side[i] = side[i] - work[i][p] * side[p]
    return side


def dot(row, column):
    terms = [a * b for a, b in zip(row, column)]
    return (terms[0] + terms[1]) + (terms[2] + terms[3]) + terms[4]


def times(matrix, vector):
    return [dot(row, vector) for row in matrix]


def product(left, right):
    columns = [[right[i][j] for i in range(NC)] for j in range(NC)]
    return [[dot(left[i], columns[j]) for j in range(NC)] for i in range(NC)]


def put(cells, value, t, place, chain, tile):
    is_a = chain == 0
    copies = [(value, 1, 0 if value < SKEW or VISC <= value < VISC + NC else 1)]
    if FLUX <= value < FLUX + NC:
        copies.append((value - FLUX + BELOW, 2, 0))
    for target, slot_a, slot_b in copies:
        if value < SKEW:
            target = jnp.where(is_a, value, value % NC * NC + value // NC)
            tile = tile * jnp.where(is_a, 1.0, -1.0).astype(jnp.float32)
        start = SUB * (SUB * t + jnp.where(is_a, slot_a, slot_b)) + 2 * place + chain
        cells[target, pl.ds(start, SUB, stride=SUB), :] = tile


def put_halo(cells, halo, place, chain):
    for value in range(VALUES):
        if value == FLUID:
            continue
        pack, slot, width = slot_of(value)
        for t in range(2):
            tile = halo[pack, pl.ds(SUB * t, SUB), :]
            if slot:
                tile = pltpu.roll(tile, LANES - slot * width, 1)
            put(cells, value, t, place, chain, tile)


def collect_kernel(bulk, sib_bulk, edge, halo_even, sib_even, halo_odd, cells):
    core = lax.axis_index("wn")
    even_place = 2 + lax.rem(lax.axis_index("az"), 2)
    for chain, array, halo in ((core, bulk, halo_even), (1 - core, sib_bulk, sib_even)):
        conv, spin, lines = parts_of(array)
        read = tile_reader(conv, spin, edge, lines)
        for value in range(VALUES):
            if value == FLUID:
                continue
            for t in range(2):
                for lt in range(2):
                    tile = mirror(read(value, t, lt), chain)
                    put(cells, value, jnp.bitwise_xor(t, chain), lt, chain, tile)
        put_halo(cells, halo, even_place, chain)
    put_halo(cells, halo_odd, 5 - even_place, core)


def main_kernel(points, *refs):
    cells, halo_odd, sib_odd, out_inc, out_defect, _ = refs[0:6]
    couple, conv_face, skews, lu, diagonal, upper_diag, lower_diag, sides, solved, vmin, vplus, azd, src, out_cells = refs[6:]

    core = lax.axis_index("wn")
    odd_place = lax.rem(lax.axis_index("az"), 2)
    row = lax.broadcasted_iota(jnp.int32, (SUB, LANES), 0)
    lane = lax.broadcasted_iota(jnp.int32, (SUB, LANES), 1)
    is_a = lax.rem(row, 2) == 0
    put_halo(cells, sib_odd, 3 - odd_place, 1 - core)

    def at(value, k):
        return cells[value, pl.ds(SUB * (k + 1), SUB), :]

    def before(x):
        y = pltpu.roll(x, S, 1)
        return jnp.where(lane < S, pltpu.roll(y, 2, 0), y)

    def after(x):
        y = pltpu.roll(x, LANES - S, 1)
        return jnp.where(lane >= LANES - S, pltpu.roll(y, SUB - 2, 0), y)

    def swap(x):
        return jnp.where(is_a, pltpu.roll(x, SUB - 1, 0), pltpu.roll(x, 1, 0))

    edges = at(EDGE, 0)

    fluid_pack, fluid_slot, fluid_width = slot_of(FLUID)
    fluid_tile = jnp.where(core == 0, halo_odd[fluid_pack, 0:SUB, :], sib_odd[fluid_pack, 0:SUB, :])
    fluid_lane = jnp.where(odd_place == 0, (fluid_slot - 1) * fluid_width, fluid_slot * fluid_width)
    fluid_tile = jnp.max(jnp.where(lane == fluid_lane, fluid_tile, 0.0), axis=1, keepdims=True)

    def fluid(k):
        return jnp.where(is_a, jnp.broadcast_to(fluid_tile[k : k + 1, :], (SUB, LANES)), 1.0)

    def edge_scale(face_a, face_b):
        face = jnp.where(is_a, float(face_a), float(face_b))
        return jnp.where(face < edges, 1.0, OUTER_SCALE)

    one = jnp.ones((SUB, LANES), jnp.float32)
    total = 2 * points
    last = points - 1
    previous = None
    for k in range(points):
        solid = k < SOLID_MOST
        if solid:
            keep = [fluid(k)] * (NC - 1) + [one]
            keep_above = [fluid(k + 1) if k + 1 < SOLID_MOST else one] * (NC - 1) + [one]
        if k < last:
            conv_out = [[at(a * NC + b, k) for b in range(NC)] for a in range(NC)]
            visc_out = [at(VISC + c, k) for c in range(NC)]
        else:
            face = [[at(a * NC + b, k) for b in range(NC)] for a in range(NC)]
            conv_out = [[jnp.where(is_a, face[a][b], -pltpu.roll(face[b][a], 1, 0)) for b in range(NC)] for a in range(NC)]
            raw = [at(VISC + c, k) for c in range(NC)]
            visc_out = [jnp.where(is_a, raw[c], pltpu.roll(raw[c], 1, 0)) for c in range(NC)]
        scale = edge_scale(k, total - 2 - k)
        visc_out = [visc_out[c] * scale for c in range(NC)]
        if solid:
            conv_out = [[conv_out[a][b] * (keep[a] * keep_above[b]) for b in range(NC)] for a in range(NC)]
            visc_out = [visc_out[c] * (keep[c] * keep_above[c]) for c in range(NC)]
        if k == 0:
            scale = edge_scale(0, total - 1)
            visc_in = [jnp.where(is_a, 0.0, at(VISC + c, -1) * scale) for c in range(NC)]

        vm, vp, az_diag, source, side = [], [], [], [], []
        for c in range(NC):
            here = at(VAZ + c, k)
            vm.append(before(here) * keep[c] if solid else before(here))
            vp.append(here * keep[c] if solid else here)
            az_diag.append(vm[c] + vp[c] + (1.0 - keep[c]) if solid else vm[c] + vp[c])
            flux_here, flux_below = at(FLUX + c, k), at(BELOW + c, k)
            if k == 0:
                flux_below = jnp.where(is_a, 0.0, flux_below)
            elif k == last:
                flux_below = jnp.where(is_a, flux_below, pltpu.roll(flux_here, 1, 0))
            flux_side = at(FAZ + c, k)
            flow = flux_below - flux_here + before(flux_side) - flux_side
            source.append(flow * keep[c] if solid else flow)
            start = at(INC + c, k)
            side.append(source[c] + (vm[c] * before(start) + vp[c] * after(start)))
            vmin[k * NC + c], vplus[k * NC + c] = vm[c], vp[c]
            azd[k * NC + c], src[k * NC + c] = az_diag[c], source[c]

        matrix = [[None] * NC for _ in range(NC)]
        for c in range(NC):
            matrix[c][c] = visc_in[c] + visc_out[c] + az_diag[c]
            diagonal[k * NC + c] = matrix[c][c]
        up = [[conv_out[a][b] - visc_out[a] if a == b else conv_out[a][b] for b in range(NC)] for a in range(NC)]
        low = [[conv_out[a][b] + visc_out[a] if a == b else conv_out[a][b] for b in range(NC)] for a in range(NC)]
        for a in range(NC):
            upper_diag[k * NC + a], lower_diag[k * NC + a] = up[a][a], low[a][a]
            for b in range(NC):
                if a != b:
                    conv_face[k * 25 + a * NC + b] = conv_out[a][b]
        if previous is not None:
            low_in, couple_in, y_in = previous
            moved = product([[low_in[b][a] for b in range(NC)] for a in range(NC)], couple_in)
            shift = times([[low_in[b][a] for b in range(NC)] for a in range(NC)], y_in)
            side = [side[c] + shift[c] for c in range(NC)]
            for c in range(NC):
                matrix[c][c] = matrix[c][c] + moved[c][c]
        for n, (a, b) in enumerate(PAIRS):
            skew = at(SKEW + n, k)
            if solid:
                skew = skew * (keep[a] * keep[b])
            skews[k * len(PAIRS) + n] = skew
            if previous is None:
                matrix[a][b], matrix[b][a] = skew, -skew
            else:
                matrix[a][b], matrix[b][a] = moved[a][b] + skew, moved[b][a] - skew
        work = factor(matrix)
        columns = [substitute(work, [up[i][j] for i in range(NC)]) for j in range(NC)]
        couple_now = [[columns[j][i] for j in range(NC)] for i in range(NC)]
        y = substitute(work, side)
        for a in range(NC):
            sides[k * NC + a] = y[a]
            for b in range(NC):
                lu[k * 25 + a * NC + b] = work[a][b]
                couple[k * 25 + a * NC + b] = couple_now[a][b]
        previous = (low, couple_now, y)
        visc_in = visc_out

    def block(ref, k):
        return [[ref[k * 25 + a * NC + b] for b in range(NC)] for a in range(NC)]

    def vector(ref, k):
        return [ref[k * NC + c] for c in range(NC)]

    def face(diagonal_ref, k):
        corner = vector(diagonal_ref, k)
        return [[corner[a] if a == b else conv_face[k * 25 + a * NC + b] for b in range(NC)] for a in range(NC)]

    def below(k, x, total=(None,) * NC):
        low, total = face(lower_diag, k - 1), list(total)
        for r in reversed(range(NC)):
            for c in range(NC):
                term = low[r][c] * x[r]
                total[c] = term if total[c] is None else total[c] + term
        return total

    couple_end = couple_now
    crossed = product(couple_end, [[swap(couple_end[a][b]) for b in range(NC)] for a in range(NC)])
    meeting = factor([[(1.0 if a == b else 0.0) - crossed[a][b] for b in range(NC)] for a in range(NC)])

    def finish(y, visit):
        shift = times(couple_end, [swap(v) for v in y])
        x = substitute(meeting, [y[c] - shift[c] for c in range(NC)])
        beyond = [swap(v) for v in x]
        for k in reversed(range(points)):
            inner = None
            if k:
                shift = times(block(couple, k - 1), x)
                y_here = vector(sides, k - 1)
                inner = [y_here[c] - shift[c] for c in range(NC)]
            visit(k, inner, x, beyond)
            x, beyond = inner, x

    def offline(k, x):
        vm, vp = vector(vmin, k), vector(vplus, k)
        return [vm[c] * before(x[c]) + vp[c] * after(x[c]) for c in range(NC)]

    def next_side(k, inner, x, beyond):
        source, moved = vector(src, k), offline(k, x)
        for c in range(NC):
            solved[k * NC + c] = source[c] + moved[c]

    def result(k, inner, x, beyond):
        source, moved, diag = vector(src, k), offline(k, x), vector(azd, k)
        main = vector(diagonal, k)
        applied = times(face(upper_diag, k), beyond)
        applied = [applied[c] + main[c] * x[c] for c in range(NC)]
        for n, (a, b) in enumerate(PAIRS):
            skew = skews[k * len(PAIRS) + n]
            applied[a] = applied[a] + skew * x[b]
            applied[b] = applied[b] - skew * x[a]
        if k:
            under = below(k, inner)
            applied = [applied[c] - under[c] for c in range(NC)]
        place = jnp.where(core == 0, k % SUB, SUB - 1 - k % SUB)
        t = jnp.where(core == 0, k // SUB, 1 - k // SUB)
        for c in range(NC):
            defect = (source[c] + moved[c] - applied[c]) / diag[c]
            out_cells[2 * c + t, pl.ds(place, SUB, stride=SUB), :] = x[c]
            out_cells[2 * (NC + c) + t, pl.ds(place, SUB, stride=SUB), :] = defect

    for sweep in range(1, SWEEPS):
        finish(y, next_side)
        for k in range(points):
            side = vector(solved, k)
            if k:
                side = below(k, y, side)
            y = substitute(block(lu, k), side)
            for c in range(NC):
                sides[k * NC + c] = y[c]
    finish(y, result)
    for c in range(NC):
        for t in range(2):
            for lt in range(2):
                start = pl.multiple_of(SUB * (2 * lt + core), SUB)
                rows, lanes = pl.ds(SUB * t, SUB), pl.ds(LANES * lt, LANES)
                out_inc[c, rows, lanes] = out_cells[2 * c + t, pl.ds(start, SUB), :]
                out_defect[c, rows, lanes] = out_cells[2 * (NC + c) + t, pl.ds(start, SUB), :]


def per_device(visc_wn, conv_wn, spin, visc_az, flux_wn, flux_az, incr_prev, cell_type, edge_index):
    components, points, line_count = visc_wn.shape
    assert components == NC and points == 2 * SUB and line_count == 2 * LANES
    count = lax.axis_size("az")
    assert count % 2 == 0
    even_pairs = [(a, a ^ 1) for a in range(count)]
    odd_pairs = [(a, (a + 1 if a % 2 else a - 1) % count) for a in range(count)]
    vmem, hbm = (pl.BlockSpec(memory_space=m) for m in (pltpu.VMEM, pltpu.HBM))

    blocks = (NC * NC, points, line_count)
    conv, spin = conv_wn.reshape(blocks), spin.reshape(blocks)
    edge = edge_index.reshape(1, line_count)
    lines = (visc_wn, flux_wn, visc_az, flux_az, incr_prev)
    pack = jax.ShapeDtypeStruct((PACKS, points, LANES), jnp.float32)
    block_array = pltpu.VMEM(blocks, jnp.float32)
    bulk = jax.ShapeDtypeStruct((2 * NC * NC + 5 * NC, points, line_count), jnp.float32)
    from_hbm = [pltpu.with_memory_space_constraint(array, pltpu.HBM) for array in (conv, spin, edge, *lines, cell_type)]
    even, odd, bulk, edge = pl.pallas_call(
        pack_kernel,
        out_shape=(pack, pack, bulk, jax.ShapeDtypeStruct((1, line_count), jnp.int32)),
        in_specs=[hbm] * 9,
        out_specs=(vmem,) * 4,
        scratch_shapes=[pltpu.SMEM((points,), jnp.int32), pltpu.SemaphoreType.DMA((NC + 4,))],
        name="pack_halo",
        compiler_params=pltpu.CompilerParams(vmem_limit_bytes=16 << 20),
    )(*from_hbm)
    halo_even = lax.ppermute(even, "az", even_pairs)
    halo_odd = lax.ppermute(odd, "az", odd_pairs)

    def cross(array):
        return lax.ppermute(array, "wn", [(0, 1), (1, 0)])

    sib_bulk = cross(bulk)
    sib_even, sib_odd = cross(halo_even), cross(halo_odd)

    tiles = jax.ShapeDtypeStruct((STORED, SLOTS * SUB, LANES), jnp.float32)
    cells = pl.pallas_call(
        collect_kernel,
        out_shape=tiles,
        in_specs=[vmem] * 6,
        out_specs=vmem,
        name="collect_lines",
        compiler_params=pltpu.CompilerParams(vmem_limit_bytes=16 << 20),
    )(bulk, sib_bulk, edge, halo_even, sib_even, halo_odd)

    def step(count):
        return pltpu.VMEM((points * count, SUB, LANES), jnp.float32)

    out = jax.ShapeDtypeStruct((NC, points, line_count), jnp.float32)
    increment, defect, _ = pl.pallas_call(
        lambda *refs: main_kernel(points, *refs),
        out_shape=(out, out, tiles),
        in_specs=[vmem] * 3,
        out_specs=(vmem, vmem, vmem),
        input_output_aliases={0: 2},
        scratch_shapes=[step(n) for n in (NC * NC, NC * NC, len(PAIRS), NC * NC)]
        + [step(NC)] * 9
        + [pltpu.VMEM((4 * NC, SUB * SUB + SUB, LANES), jnp.float32)],
        name="relax_lines",
        compiler_params=pltpu.CompilerParams(vmem_limit_bytes=24 << 20),
    )(cells, halo_odd, sib_odd)
    return increment, defect


def solution(mesh):
    in_specs = (
        P(None, "wn", "az"),
        P(None, None, "wn", "az"),
        P(None, None, "wn", "az"),
        P(None, "wn", "az"),
        P(None, "wn", "az"),
        P(None, "wn", "az"),
        P(None, "wn", "az"),
        P("wn"),
        P("az"),
    )
    out_specs = (P(None, "wn", "az"), P(None, "wn", "az"))
    return jax.shard_map(
        per_device, mesh=mesh, in_specs=in_specs, out_specs=out_specs, check_vma=False
    )
```

```python
import jax
import jax.numpy as jnp
from jax import lax
from jax.experimental import pallas as pl
from jax.experimental.pallas import tpu as pltpu
from jax.sharding import PartitionSpec as P

S = 8
SWEEPS = 2
OUTER_SCALE = 0.25
NC = 5
LANES = 128
SUB = 8
NEAR = 2 * S
FAR = 3 * S

CONV, SKEW, VISC, FLUX, EDGE, FLUID = 0, 25, 35, 40, 45, 46
NEAR_VALUES = 47
VAZ, FAZ, INC = 47, 52, 57
VALUES = 62
BELOW, STORED = 62, 67
SLOTS = 19
SOLID_MOST = 4
NEAR_SLOTS = LANES // NEAR
FAR_SLOTS = LANES // FAR
NEAR_PACKS = -(-NEAR_VALUES // NEAR_SLOTS)
FAR_PACKS = -(-(VALUES - NEAR_VALUES) // FAR_SLOTS)
PACKS = NEAR_PACKS + FAR_PACKS
PAIRS = [(a, b) for a in range(NC) for b in range(a + 1, NC)]


def slot_of(value):
    if value < NEAR_VALUES:
        return value // NEAR_SLOTS, value % NEAR_SLOTS, NEAR
    other = value - NEAR_VALUES
    return NEAR_PACKS + other // FAR_SLOTS, other % FAR_SLOTS, FAR


def tile_reader(conv, spin, edge, lines):
    def read(value, t, lt):
        rows, lanes = pl.ds(SUB * t, SUB), pl.ds(LANES * lt, LANES)
        if value < SKEW:
            return conv[value, rows, lanes]
        if value < VISC:
            a, b = PAIRS[value - SKEW]
            return spin[a * NC + b, rows, lanes] - spin[b * NC + a, rows, lanes]
        if value == EDGE:
            return jnp.broadcast_to(edge[0:1, lanes].astype(jnp.float32), (SUB, LANES))
        for first, ref in zip((VISC, FLUX, VAZ, FAZ, INC), lines):
            if first <= value < first + NC:
                return ref[value - first, rows, lanes]

    return read


def parts_of(ref):
    lines = [ref.at[pl.ds(2 * NC * NC + NC * n, NC)] for n in range(5)]
    return ref.at[pl.ds(0, NC * NC)], ref.at[pl.ds(NC * NC, NC * NC)], lines


def mirror(tile, chain):
    row = lax.broadcasted_iota(jnp.int32, (SUB, LANES), 0)
    return jnp.take_along_axis(tile, jnp.where(chain == 0, row, SUB - 1 - row), axis=0)


def pack_kernel(conv_hbm, spin_hbm, edge_hbm, visc_hbm, flux_hbm, vaz_hbm, faz_hbm, inc_hbm, cells_hbm,
                even_out, odd_out, bulk, edge, cells, sems):
    odd_place = lax.rem(lax.axis_index("az"), 2) == 1
    core = lax.axis_index("wn")
    conv, spin, lines = parts_of(bulk)
    copies = []
    copies.append(pltpu.make_async_copy(conv_hbm, conv, sems.at[0]))
    for n, ref in enumerate((visc_hbm, flux_hbm, vaz_hbm, faz_hbm, inc_hbm)):
        copies.append(pltpu.make_async_copy(ref, lines[n], sems.at[1 + n]))
    copies.append(pltpu.make_async_copy(spin_hbm, spin, sems.at[NC + 1]))
    copies.append(pltpu.make_async_copy(edge_hbm, edge, sems.at[NC + 2]))
    copies.append(pltpu.make_async_copy(cells_hbm, cells, sems.at[NC + 3]))
    for copy in copies:
        copy.start()
    read = tile_reader(conv, spin, edge, lines)
    lane = lax.broadcasted_iota(jnp.int32, (SUB, LANES), 1)
    row = lax.broadcasted_iota(jnp.int32, (SUB, LANES), 0)
    blank = jnp.zeros((SUB, LANES), jnp.float32)
    first = [[blank] * PACKS for _ in range(2)]
    last = [[blank] * PACKS for _ in range(2)]
    late = list(range(SKEW, VISC)) + [EDGE, FLUID]
    for value in [v for v in range(VALUES) if v not in late] + late:
        for group, begin in enumerate([CONV, VISC, FLUX, VAZ, FAZ, INC]):
            if value == begin:
                copies[group].wait()
        if value == late[0]:
            for copy in copies[NC + 1 :]:
                copy.wait()
        pack, slot, width = slot_of(value)
        low = slot * width
        here = (lane >= low) & (lane < low + width)
        low = (LANES - width + slot * width) % LANES
        there = (lane >= low) & (lane < low + width)
        for t in range(2):
            if value == FLUID:
                one = jnp.ones((SUB, LANES), jnp.float32)
                for p in range(SOLID_MOST if t == 0 else 0):
                    one = jnp.where(row == p, jnp.where(cells[p] == 0, 1.0, 0.0).astype(jnp.float32), one)
                two = one
            else:
                one = jnp.where(lane < LANES // 2, read(value, t, 0), read(value, t, 1))
                if slot:
                    one = pltpu.roll(one, slot * width, 1)
                two = one
            first[t][pack] = jnp.where(here, one, first[t][pack])
            last[t][pack] = jnp.where(there, two, last[t][pack])
    for pack in range(PACKS):
        for t in range(2):
            rows = pl.ds(SUB * t, SUB)
            one = mirror(jnp.where(core == 0, first[t][pack], first[1 - t][pack]), core)
            two = mirror(jnp.where(core == 0, last[t][pack], last[1 - t][pack]), core)
            even_out[pack, rows, :] = jnp.where(odd_place, one, two)
            odd_out[pack, rows, :] = jnp.where(odd_place, two, one)


def factor(matrix):
    work = [list(row) for row in matrix]
    scale = []
    for p in range(NC):
        scale.append(1.0 / work[p][p])
        for i in range(p + 1, NC):
            work[i][p] = work[i][p] * scale[p]
            for j in range(p + 1, NC):
                work[i][j] = work[i][j] - work[i][p] * work[p][j]
    for p in range(NC):
        work[p][p] = scale[p]
        for j in range(p + 1, NC):
            work[p][j] = work[p][j] * scale[p]
    return work


def substitute(work, side):
    side = list(side)
    for p in range(NC):
        for i in range(p + 1, NC):
            side[i] = side[i] - work[i][p] * side[p]
    side = [side[p] * work[p][p] for p in range(NC)]
    for p in reversed(range(NC)):
        for i in range(p):
            side[i] = side[i] - work[i][p] * side[p]
    return side


def dot(row, column):
    terms = [a * b for a, b in zip(row, column)]
    return (terms[0] + terms[1]) + (terms[2] + terms[3]) + terms[4]


def times(matrix, vector):
    return [dot(row, vector) for row in matrix]


def product(left, right):
    columns = [[right[i][j] for i in range(NC)] for j in range(NC)]
    return [[dot(left[i], columns[j]) for j in range(NC)] for i in range(NC)]


def put(cells, value, t, place, chain, tile):
    is_a = chain == 0
    copies = [(value, 1, 0 if value < SKEW or VISC <= value < VISC + NC else 1)]
    if FLUX <= value < FLUX + NC:
        copies.append((value - FLUX + BELOW, 2, 0))
    for target, slot_a, slot_b in copies:
        if value < SKEW:
            target = jnp.where(is_a, value, value % NC * NC + value // NC)
            tile = tile * jnp.where(is_a, 1.0, -1.0).astype(jnp.float32)
        start = SUB * (SUB * t + jnp.where(is_a, slot_a, slot_b)) + 2 * place + chain
        cells[target, pl.ds(start, SUB, stride=SUB), :] = tile


def put_halo(cells, halo, place, chain):
    for value in range(VALUES):
        if value == FLUID:
            continue
        pack, slot, width = slot_of(value)
        for t in range(2):
            tile = halo[pack, pl.ds(SUB * t, SUB), :]
            if slot:
                tile = pltpu.roll(tile, LANES - slot * width, 1)
            put(cells, value, t, place, chain, tile)


def collect_kernel(bulk, sib_bulk, edge, halo_even, sib_even, halo_odd, cells):
    core = lax.axis_index("wn")
    even_place = 2 + lax.rem(lax.axis_index("az"), 2)
    for chain, array, halo in ((core, bulk, halo_even), (1 - core, sib_bulk, sib_even)):
        conv, spin, lines = parts_of(array)
        read = tile_reader(conv, spin, edge, lines)
        for value in range(VALUES):
            if value == FLUID:
                continue
            for t in range(2):
                for lt in range(2):
                    tile = mirror(read(value, t, lt), chain)
                    put(cells, value, jnp.bitwise_xor(t, chain), lt, chain, tile)
        put_halo(cells, halo, even_place, chain)
    put_halo(cells, halo_odd, 5 - even_place, core)


def main_kernel(points, *refs):
    cells, halo_odd, sib_odd, out_inc, out_defect, _ = refs[0:6]
    couple, conv_face, skews, lu, diagonal, upper_diag, lower_diag, sides, solved, vmin, vplus, azd, src, out_cells = refs[6:]

    core = lax.axis_index("wn")
    odd_place = lax.rem(lax.axis_index("az"), 2)
    row = lax.broadcasted_iota(jnp.int32, (SUB, LANES), 0)
    lane = lax.broadcasted_iota(jnp.int32, (SUB, LANES), 1)
    is_a = lax.rem(row, 2) == 0
    put_halo(cells, sib_odd, 3 - odd_place, 1 - core)

    def at(value, k):
        return cells[value, pl.ds(SUB * (k + 1), SUB), :]

    def before(x):
        y = pltpu.roll(x, S, 1)
        return jnp.where(lane < S, pltpu.roll(y, 2, 0), y)

    def after(x):
        y = pltpu.roll(x, LANES - S, 1)
        return jnp.where(lane >= LANES - S, pltpu.roll(y, SUB - 2, 0), y)

    def swap(x):
        return jnp.where(is_a, pltpu.roll(x, SUB - 1, 0), pltpu.roll(x, 1, 0))

    edges = at(EDGE, 0)

    fluid_pack, fluid_slot, fluid_width = slot_of(FLUID)
    fluid_tile = jnp.where(core == 0, halo_odd[fluid_pack, 0:SUB, :], sib_odd[fluid_pack, 0:SUB, :])
    fluid_lane = jnp.where(odd_place == 0, (fluid_slot - 1) * fluid_width, fluid_slot * fluid_width)
    fluid_tile = jnp.max(jnp.where(lane == fluid_lane, fluid_tile, 0.0), axis=1, keepdims=True)

    def fluid(k):
        return jnp.where(is_a, jnp.broadcast_to(fluid_tile[k : k + 1, :], (SUB, LANES)), 1.0)

    def edge_scale(face_a, face_b):
        face = jnp.where(is_a, float(face_a), float(face_b))
        return jnp.where(face < edges, 1.0, OUTER_SCALE)

    one = jnp.ones((SUB, LANES), jnp.float32)
    total = 2 * points
    last = points - 1
    previous = None
    for k in range(points):
        solid = k < SOLID_MOST
        if solid:
            keep = [fluid(k)] * (NC - 1) + [one]
            keep_above = [fluid(k + 1) if k + 1 < SOLID_MOST else one] * (NC - 1) + [one]
        if k < last:
            conv_out = [[at(a * NC + b, k) for b in range(NC)] for a in range(NC)]
            visc_out = [at(VISC + c, k) for c in range(NC)]
        else:
            face = [[at(a * NC + b, k) for b in range(NC)] for a in range(NC)]
            conv_out = [[jnp.where(is_a, face[a][b], -pltpu.roll(face[b][a], 1, 0)) for b in range(NC)] for a in range(NC)]
            raw = [at(VISC + c, k) for c in range(NC)]
            visc_out = [jnp.where(is_a, raw[c], pltpu.roll(raw[c], 1, 0)) for c in range(NC)]
        scale = edge_scale(k, total - 2 - k)
        visc_out = [visc_out[c] * scale for c in range(NC)]
        if solid:
            conv_out = [[conv_out[a][b] * (keep[a] * keep_above[b]) for b in range(NC)] for a in range(NC)]
            visc_out = [visc_out[c] * (keep[c] * keep_above[c]) for c in range(NC)]
        if k == 0:
            scale = edge_scale(0, total - 1)
            visc_in = [jnp.where(is_a, 0.0, at(VISC + c, -1) * scale) for c in range(NC)]

        vm, vp, az_diag, source, side = [], [], [], [], []
        for c in range(NC):
            here = at(VAZ + c, k)
            vm.append(before(here) * keep[c] if solid else before(here))
            vp.append(here * keep[c] if solid else here)
            az_diag.append(vm[c] + vp[c] + (1.0 - keep[c]) if solid else vm[c] + vp[c])
            flux_here, flux_below = at(FLUX + c, k), at(BELOW + c, k)
            if k == 0:
                flux_below = jnp.where(is_a, 0.0, flux_below)
            elif k == last:
                flux_below = jnp.where(is_a, flux_below, pltpu.roll(flux_here, 1, 0))
            flux_side = at(FAZ + c, k)
            flow = flux_below - flux_here + before(flux_side) - flux_side
            source.append(flow * keep[c] if solid else flow)
            start = at(INC + c, k)
            side.append(source[c] + (vm[c] * before(start) + vp[c] * after(start)))
            vmin[k * NC + c], vplus[k * NC + c] = vm[c], vp[c]
            azd[k * NC + c], src[k * NC + c] = az_diag[c], source[c]

        matrix = [[None] * NC for _ in range(NC)]
        for c in range(NC):
            matrix[c][c] = visc_in[c] + visc_out[c] + az_diag[c]
            diagonal[k * NC + c] = matrix[c][c]
        up = [[conv_out[a][b] - visc_out[a] if a == b else conv_out[a][b] for b in range(NC)] for a in range(NC)]
        low = [[conv_out[a][b] + visc_out[a] if a == b else conv_out[a][b] for b in range(NC)] for a in range(NC)]
        for a in range(NC):
            upper_diag[k * NC + a], lower_diag[k * NC + a] = up[a][a], low[a][a]
            for b in range(NC):
                if a != b:
                    conv_face[k * 25 + a * NC + b] = conv_out[a][b]
        if previous is not None:
            low_in, couple_in, y_in = previous
            moved = product([[low_in[b][a] for b in range(NC)] for a in range(NC)], couple_in)
            shift = times([[low_in[b][a] for b in range(NC)] for a in range(NC)], y_in)
            side = [side[c] + shift[c] for c in range(NC)]
            for c in range(NC):
                matrix[c][c] = matrix[c][c] + moved[c][c]
        for n, (a, b) in enumerate(PAIRS):
            skew = at(SKEW + n, k)
            if solid:
                skew = skew * (keep[a] * keep[b])
            skews[k * len(PAIRS) + n] = skew
            if previous is None:
                matrix[a][b], matrix[b][a] = skew, -skew
            else:
                matrix[a][b], matrix[b][a] = moved[a][b] + skew, moved[b][a] - skew
        work = factor(matrix)
        columns = [substitute(work, [up[i][j] for i in range(NC)]) for j in range(NC)]
        couple_now = [[columns[j][i] for j in range(NC)] for i in range(NC)]
        y = substitute(work, side)
        for a in range(NC):
            sides[k * NC + a] = y[a]
            for b in range(NC):
                lu[k * 25 + a * NC + b] = work[a][b]
                couple[k * 25 + a * NC + b] = couple_now[a][b]
        previous = (low, couple_now, y)
        visc_in = visc_out

    def block(ref, k):
        return [[ref[k * 25 + a * NC + b] for b in range(NC)] for a in range(NC)]

    def vector(ref, k):
        return [ref[k * NC + c] for c in range(NC)]

    def face(diagonal_ref, k):
        corner = vector(diagonal_ref, k)
        return [[corner[a] if a == b else conv_face[k * 25 + a * NC + b] for b in range(NC)] for a in range(NC)]

    def below(k, x, total=(None,) * NC):
        low, total = face(lower_diag, k - 1), list(total)
        for r in reversed(range(NC)):
            for c in range(NC):
                term = low[r][c] * x[r]
                total[c] = term if total[c] is None else total[c] + term
        return total

    couple_end = couple_now
    crossed = product(couple_end, [[swap(couple_end[a][b]) for b in range(NC)] for a in range(NC)])
    meeting = factor([[(1.0 if a == b else 0.0) - crossed[a][b] for b in range(NC)] for a in range(NC)])

    def finish(y, visit):
        shift = times(couple_end, [swap(v) for v in y])
        x = substitute(meeting, [y[c] - shift[c] for c in range(NC)])
        beyond = [swap(v) for v in x]
        for k in reversed(range(points)):
            inner = None
            if k:
                y_here, inner = vector(sides, k - 1), []
                for c, row_c in enumerate(block(couple, k - 1)):
                    terms = [row_c[r] * x[r] for r in range(NC)]
                    inner.append(((y_here[c] - terms[0]) - (terms[1] + terms[2])) - (terms[3] + terms[4]))
            visit(k, inner, x, beyond)
            x, beyond = inner, x

    def offline(k, x):
        vm, vp = vector(vmin, k), vector(vplus, k)
        return [vm[c] * before(x[c]) + vp[c] * after(x[c]) for c in range(NC)]

    def next_side(k, inner, x, beyond):
        source, moved = vector(src, k), offline(k, x)
        for c in range(NC):
            solved[k * NC + c] = source[c] + moved[c]

    def result(k, inner, x, beyond):
        source, moved, diag = vector(src, k), offline(k, x), vector(azd, k)
        main = vector(diagonal, k)
        applied = times(face(upper_diag, k), beyond)
        applied = [applied[c] + main[c] * x[c] for c in range(NC)]
        for n, (a, b) in enumerate(PAIRS):
            skew = skews[k * len(PAIRS) + n]
            applied[a] = applied[a] + skew * x[b]
            applied[b] = applied[b] - skew * x[a]
        if k:
            under = below(k, inner)
            applied = [applied[c] - under[c] for c in range(NC)]
        place = jnp.where(core == 0, k % SUB, SUB - 1 - k % SUB)
        t = jnp.where(core == 0, k // SUB, 1 - k // SUB)
        for c in range(NC):
            defect = (source[c] + moved[c] - applied[c]) / diag[c]
            out_cells[2 * c + t, pl.ds(place, SUB, stride=SUB), :] = x[c]
            out_cells[2 * (NC + c) + t, pl.ds(place, SUB, stride=SUB), :] = defect

    for sweep in range(1, SWEEPS):
        finish(y, next_side)
        for k in range(points):
            side = vector(solved, k)
            if k:
                side = below(k, y, side)
            y = substitute(block(lu, k), side)
            for c in range(NC):
                sides[k * NC + c] = y[c]
    finish(y, result)
    for c in range(NC):
        for t in range(2):
            for lt in range(2):
                start = pl.multiple_of(SUB * (2 * lt + core), SUB)
                rows, lanes = pl.ds(SUB * t, SUB), pl.ds(LANES * lt, LANES)
                out_inc[c, rows, lanes] = out_cells[2 * c + t, pl.ds(start, SUB), :]
                out_defect[c, rows, lanes] = out_cells[2 * (NC + c) + t, pl.ds(start, SUB), :]


def per_device(visc_wn, conv_wn, spin, visc_az, flux_wn, flux_az, incr_prev, cell_type, edge_index):
    components, points, line_count = visc_wn.shape
    assert components == NC and points == 2 * SUB and line_count == 2 * LANES
    count = lax.axis_size("az")
    assert count % 2 == 0
    even_pairs = [(a, a ^ 1) for a in range(count)]
    odd_pairs = [(a, (a + 1 if a % 2 else a - 1) % count) for a in range(count)]
    vmem, hbm = (pl.BlockSpec(memory_space=m) for m in (pltpu.VMEM, pltpu.HBM))

    blocks = (NC * NC, points, line_count)
    conv, spin = conv_wn.reshape(blocks), spin.reshape(blocks)
    edge = edge_index.reshape(1, line_count)
    lines = (visc_wn, flux_wn, visc_az, flux_az, incr_prev)
    pack = jax.ShapeDtypeStruct((PACKS, points, LANES), jnp.float32)
    block_array = pltpu.VMEM(blocks, jnp.float32)
    bulk = jax.ShapeDtypeStruct((2 * NC * NC + 5 * NC, points, line_count), jnp.float32)
    from_hbm = [pltpu.with_memory_space_constraint(array, pltpu.HBM) for array in (conv, spin, edge, *lines, cell_type)]
    even, odd, bulk, edge = pl.pallas_call(
        pack_kernel,
        out_shape=(pack, pack, bulk, jax.ShapeDtypeStruct((1, line_count), jnp.int32)),
        in_specs=[hbm] * 9,
        out_specs=(vmem,) * 4,
        scratch_shapes=[pltpu.SMEM((points,), jnp.int32), pltpu.SemaphoreType.DMA((NC + 4,))],
        name="pack_halo",
        compiler_params=pltpu.CompilerParams(vmem_limit_bytes=16 << 20),
    )(*from_hbm)
    halo_even = lax.ppermute(even, "az", even_pairs)
    halo_odd = lax.ppermute(odd, "az", odd_pairs)

    def cross(array):
        return lax.ppermute(array, "wn", [(0, 1), (1, 0)])

    sib_bulk = cross(bulk)
    sib_even, sib_odd = cross(halo_even), cross(halo_odd)

    tiles = jax.ShapeDtypeStruct((STORED, SLOTS * SUB, LANES), jnp.float32)
    cells = pl.pallas_call(
        collect_kernel,
        out_shape=tiles,
        in_specs=[vmem] * 6,
        out_specs=vmem,
        name="collect_lines",
        compiler_params=pltpu.CompilerParams(vmem_limit_bytes=16 << 20),
    )(bulk, sib_bulk, edge, halo_even, sib_even, halo_odd)

    def step(count):
        return pltpu.VMEM((points * count, SUB, LANES), jnp.float32)

    out = jax.ShapeDtypeStruct((NC, points, line_count), jnp.float32)
    increment, defect, _ = pl.pallas_call(
        lambda *refs: main_kernel(points, *refs),
        out_shape=(out, out, tiles),
        in_specs=[vmem] * 3,
        out_specs=(vmem, vmem, vmem),
        input_output_aliases={0: 2},
        scratch_shapes=[step(n) for n in (NC * NC, NC * NC, len(PAIRS), NC * NC)]
        + [step(NC)] * 9
        + [pltpu.VMEM((4 * NC, SUB * SUB + SUB, LANES), jnp.float32)],
        name="relax_lines",
        compiler_params=pltpu.CompilerParams(vmem_limit_bytes=24 << 20),
    )(cells, halo_odd, sib_odd)
    return increment, defect


def solution(mesh):
    in_specs = (
        P(None, "wn", "az"),
        P(None, None, "wn", "az"),
        P(None, None, "wn", "az"),
        P(None, "wn", "az"),
        P(None, "wn", "az"),
        P(None, "wn", "az"),
        P(None, "wn", "az"),
        P("wn"),
        P("az"),
    )
    out_specs = (P(None, "wn", "az"), P(None, "wn", "az"))
    return jax.shard_map(
        per_device, mesh=mesh, in_specs=in_specs, out_specs=out_specs, check_vma=False
    )
```
